256 devices in a mesh: rows: 16 (over z, core), strata: 16 (over y, x).
Axes of the slice: x: 4, y: 4, z: 8, core: 2. Of those that a mesh axis runs over, the one named last changes fastest.
Arguments:
- user_factors: float32 [32768, 512], P(('rows', 'strata')), may hold values from -1.3 to 1.3
- item_factors: float32 [131072, 512], P(('rows', 'strata')), may hold values from -1.3 to 1.3
- ratings: float32 [2, 262144], P(None, ('rows', 'strata')), may hold values from -6 to 6
- user_offsets: int32 [2, 262144], P(None, ('rows', 'strata')), may hold values from 0 to 2047, as said below
- item_offsets: int32 [2, 262144], P(None, ('rows', 'strata')), may hold values from 0 to 511
- counts: int32 [2, 256], P(None, ('rows', 'strata')), may hold values from 128 to 1024, as said below
Outputs:
- new_users: float32 [32768, 512], P(('rows', 'strata'))
- new_items: float32 [131072, 512], P(('rows', 'strata'))
The draws below stay inside these ranges and needn't reach their ends.
Inputs may be any that keep to these rules, and one draw needn't show every extreme that they name: `counts`: some tile of each sub-epoch has all 1024 slots active. `user_offsets`: splitting a user block into 16 runs of 128 users, each tile's slots (active or not) name exactly 32 distinct users of every run.
All inputs are finite; a program needn't handle non-finite values.
Results may differ from the reference program's by a relative error of at most 0.0003.
Values sent between devices are 32-bit elements; how exact they have to be, the bound alone decides.
A program may use at most 64 MiB of HBM per device.

```python
import jax
import jax.numpy as jnp
from jax import lax

K = 512
USER_DEV = 128
TILE_COLS = 512
ENTRIES = 1024
SUBS = 2
TOUCH = 32
USERS = 32768
ITEMS = 131072
N_ROWS = 16
N_STRATA = 16


def draw_counts(key, part):
    first_key = jax.random.fold_in(key, 11)
    second_key = jax.random.fold_in(key, 23)
    device_count = N_ROWS * N_STRATA
    halvings = jax.random.randint(first_key, (SUBS, device_count), 0, 4)
    loads = jnp.right_shift(jnp.full((SUBS, device_count), ENTRIES, jnp.int32), halvings)
    chosen = jax.random.randint(second_key, (SUBS, 1), 0, device_count)
    places = jnp.arange(device_count, dtype=jnp.int32)[None, :]
    return jnp.where(places == chosen, ENTRIES, loads).astype(jnp.int32)


def draw_user_offsets(key, part):
    pick_key = jax.random.fold_in(key, 31)
    order_key = jax.random.fold_in(key, 37)
    fill_key = jax.random.fold_in(key, 41)
    tiles = N_ROWS * N_STRATA
    pairs = N_STRATA * TOUCH
    pick_keys = jax.random.split(pick_key, SUBS * tiles * N_STRATA)
    chosen = jax.vmap(lambda k: jax.random.permutation(k, USER_DEV)[:TOUCH])(pick_keys)
    chosen = chosen.reshape(SUBS, tiles, N_STRATA, TOUCH)
    chosen = chosen + (jnp.arange(N_STRATA, dtype=jnp.int32) * USER_DEV)[None, None, :, None]
    chosen = chosen.reshape(SUBS, tiles, pairs).astype(jnp.int32)
    extra = jax.random.randint(fill_key, (SUBS, tiles, ENTRIES), 0, pairs)
    slots = jnp.arange(ENTRIES, dtype=jnp.int32)[None, None, :]
    base = jnp.where(slots < pairs, slots % pairs, extra).astype(jnp.int32)
    order_keys = jax.random.split(order_key, SUBS * tiles)
    orders = jax.vmap(lambda k: jax.random.permutation(k, ENTRIES))(order_keys).reshape(SUBS, tiles, ENTRIES)
    pair_ids = jnp.take_along_axis(base, orders.astype(jnp.int32), axis=2)
    users = jnp.take_along_axis(chosen, pair_ids, axis=2)
    return users.reshape(SUBS, tiles * ENTRIES).astype(jnp.int32)


def with_ends(values, rng, least, top_value):
    longest = values.shape.index(max(values.shape))
    spots = []
    for shift in (0, 1):
        where = [jax.random.randint(jax.random.fold_in(rng, axis), (), 0, length) for axis, length in enumerate(values.shape)]
        where[longest] = (where[longest] + shift) % values.shape[longest]
        spots.append(tuple(where))
    return values.at[spots[0]].set(least).at[spots[1]].set(top_value)


def block_scale(own_key, dims, shards, least, largest):
    def one(axis_at, shards_of):
        steps = jax.random.uniform(jax.random.fold_in(jax.random.fold_in(own_key, 6), axis_at), (shards_of,), jnp.float32, least / len(shards), largest / len(shards))
        return jnp.repeat(jnp.exp(steps), dims[axis_at] // shards_of).reshape((-1,) + (1,) * (len(dims) - axis_at - 1))

    gain = one(*shards[0])
    for cut in shards[1:]:
        gain = gain * one(*cut)
    return gain


def gaussian(own_key, shape, deviation, limit, shards=(), held_as=jnp.bfloat16):
    values = deviation * jax.random.normal(own_key, shape, jnp.float32)
    if shards:
        values = values * block_scale(own_key, shape, shards, -0.22, 0.18)
    return jnp.clip(values, -limit, limit).astype(held_as)


def setup_inputs(seed: int = 0) -> dict:
    splits = jax.random.split(jax.random.key(seed), 7)
    return {
        "user_factors": gaussian(splits[0], (USERS, K), 0.21, 1.3, ((0, 256),), jnp.float32),
        "item_factors": gaussian(splits[1], (ITEMS, K), 0.21, 1.3, ((0, 256),), jnp.float32),
        "ratings": gaussian(splits[2], (SUBS, N_ROWS * N_STRATA * ENTRIES), 1.0, 6.0, ((1, 256),), jnp.float32),
        "user_offsets": draw_user_offsets(jax.random.fold_in(splits[6], 71), 0),
        "item_offsets": with_ends(jax.random.randint(splits[4], (SUBS, N_ROWS * N_STRATA * ENTRIES), 0, TILE_COLS), jax.random.fold_in(splits[4], 1), 0, TILE_COLS - 1).astype(jnp.int32),
        "counts": draw_counts(jax.random.fold_in(splits[6], 71), 0),
    }


def reference(user_factors, item_factors, ratings, user_offsets, item_offsets, counts):
    device_count = N_ROWS * N_STRATA
    user_block = USER_DEV * N_STRATA
    user_table = user_factors
    item_table = item_factors
    for sub_epoch in range(SUBS):
        def tile_step(totals, device):
            grad_u, grad_v = totals
            row_pos = device // N_STRATA
            strat_pos = device % N_STRATA
            col_block = ((row_pos - sub_epoch) % N_ROWS) * N_STRATA + strat_pos
            first_slot = (device * ENTRIES).astype(jnp.int32)
            user_index = row_pos * user_block + lax.dynamic_slice_in_dim(user_offsets[sub_epoch], first_slot, ENTRIES)
            item_index = col_block * TILE_COLS + lax.dynamic_slice_in_dim(item_offsets[sub_epoch], first_slot, ENTRIES)
            observed = lax.dynamic_slice_in_dim(ratings[sub_epoch], first_slot, ENTRIES)
            active_mask = (jnp.arange(ENTRIES, dtype=jnp.int32) < counts[sub_epoch, device]).astype(jnp.float32)
            u_rows = user_table[user_index]
            v_rows = item_table[item_index]
            errors = active_mask * (observed - jnp.sum(u_rows * v_rows, axis=1))
            grad_u = grad_u.at[user_index].add(errors[:, None] * v_rows)
            grad_v = grad_v.at[item_index].add(errors[:, None] * u_rows)
            return (grad_u, grad_v), None

        start = (jnp.zeros_like(user_table), jnp.zeros_like(item_table))
        (grad_u, grad_v), _ = lax.scan(tile_step, start, jnp.arange(device_count, dtype=jnp.int32))
        step_size = 0.04 / (1.0 + 0.5 * sub_epoch)
        user_table = user_table + step_size * (grad_u - 0.1 * user_table)
        item_table = item_table + step_size * (grad_v - 0.1 * item_table)
    return user_table, item_table
```

```python
import functools

import jax
import jax.numpy as jnp
from jax import lax
from jax.experimental import pallas as pl
from jax.experimental.pallas import tpu as pltpu
from jax.sharding import PartitionSpec as P

MESH = pl.DeviceIdType.MESH
F32 = jnp.float32
BF16 = jnp.bfloat16

SIDE = 4
OWNERS = SIDE * SIDE
RUN = 128
TOUCH = 32
GROUPS = SIDE
ORDER = (0, 1, 3, 2)

NN = (((1,), (0,)), ((), ()))
NT = (((1,), (1,)), ((), ()))
TN = (((0,), (0,)), ((), ()))


def mm(a, b, dims):
    return lax.dot_general(a, b, dims, preferred_element_type=F32)


def halves(value):
    top = value.astype(BF16)
    return top, (value - top.astype(F32)).astype(BF16)


def mm3(a, b, dims):
    return mm(a[0], b[0], dims) + mm(a[0], b[1], dims) + mm(a[1], b[0], dims)


def iota(shape, dim):
    return lax.broadcasted_iota(jnp.int32, shape, dim)


def onehot(test):
    return jnp.where(test, 1.0, 0.0).astype(BF16)


def steps_of(sub_epoch):
    return 0.04 / (1.0 + 0.5 * sub_epoch)


def kernel(
    n_rows,
    u_hbm, v_hbm, rate_ref, user_ref, item_ref, count_ref,
    out_u, out_v,
    u_own, v_cur, v_new, v_hi, v_lo,
    mask_send, mask_recv, rank_tab, pos_tab,
    sel, sel_t,
    b_one, b_hi, b_lo, num, rat,
    ut_hi, ut_lo, w_hi, w_lo,
    u_send, u_recv, g_send, g_recv, u_parts,
    load_sem, mask_ss, mask_rs, u_ss, u_rs, g_ss, g_rs, v_ss, v_rs,
):
    row = lax.axis_index("rows")
    place = lax.axis_index("strata")
    y, x = place // SIDE, place % SIDE
    up, down = (row + 1) % n_rows, (row + n_rows - 1) % n_rows
    items = v_cur.shape[0]
    entries = rate_ref.shape[1]
    subs = rate_ref.shape[0]

    def away(slot, sign):
        dy, dx = slot // SIDE, slot % SIDE
        return ((y + sign * dy + SIDE) % SIDE) * SIDE + (x + sign * dx + SIDE) % SIDE

    def tile_of(slot):
        return (row, away(slot, 1))

    def owner_of(slot):
        return (row, away(slot, -1))

    barrier = pltpu.get_barrier_semaphore()
    for slot in range(1, OWNERS):
        pl.semaphore_signal(barrier, inc=1, device_id=tile_of(slot), device_id_type=MESH)
    for other in (up, down):
        pl.semaphore_signal(barrier, inc=1, device_id=(other, place), device_id_type=MESH)

    load_u = pltpu.make_async_copy(u_hbm, u_own, load_sem.at[0])
    load_v = pltpu.make_async_copy(v_hbm, v_cur, load_sem.at[1])
    load_u.start()
    load_v.start()

    def slot_and_run(t):
        user = user_ref[t : t + 1, :]
        owner = user >> 7
        dy = (y + SIDE - (owner >> 2)) & 3
        dx = (x + SIDE - (owner & 3)) & 3
        return dy * SIDE + dx, user & (RUN - 1)

    for t in range(subs):
        slot_e, low_e = slot_and_run(t)
        hot_slot = onehot(iota((OWNERS, entries), 0) == slot_e)
        hot_low = onehot(iota((RUN, entries), 0) == low_e)
        named = jnp.where(mm(hot_slot, hot_low, NT) > 0.5, 1.0, 0.0)
        mask_send[:, t, :] = named
        before = onehot(iota((RUN, RUN), 0) < iota((RUN, RUN), 1))
        rank = mm(named.astype(BF16), before, NN)
        each = mm(rank.astype(BF16), hot_low, NN)
        rank_e = jnp.sum(jnp.where(iota((OWNERS, entries), 0) == slot_e, each, 0.0), axis=0, keepdims=True)
        pos_tab[t : t + 1, :] = slot_e.astype(F32) * float(TOUCH) + rank_e

    pl.semaphore_wait(barrier, OWNERS + 1)

    def mask_copy(slot):
        return pltpu.make_async_remote_copy(
            src_ref=mask_send.at[slot], dst_ref=mask_recv.at[slot],
            send_sem=mask_ss.at[slot], recv_sem=mask_rs.at[slot],
            device_id=owner_of(slot), device_id_type=MESH)

    def u_copy(t, slot):
        return pltpu.make_async_remote_copy(
            src_ref=u_send.at[t, slot], dst_ref=u_recv.at[t, slot],
            send_sem=u_ss.at[t, slot], recv_sem=u_rs.at[t, slot],
            device_id=tile_of(slot), device_id_type=MESH)

    def g_copy(t, slot):
        return pltpu.make_async_remote_copy(
            src_ref=g_send.at[t, slot], dst_ref=g_recv.at[t, slot],
            send_sem=g_ss.at[t, slot], recv_sem=g_rs.at[t, slot],
            device_id=owner_of(slot), device_id_type=MESH)

    def slots_of(group):
        return range(group * SIDE, (group + 1) * SIDE)

    def rows_of(group):
        return slice(group * RUN, (group + 1) * RUN)

    for group in ORDER:
        for slot in slots_of(group):
            if slot:
                mask_copy(slot).start()
    mask_recv[0] = mask_send[0]

    load_u.wait()
    top, low = halves(u_own[...])
    u_parts[0] = top
    u_parts[1] = low

    def one_hot_items(t):
        active = iota((1, entries), 1) < count_ref[t : t + 1, 0:1]
        rate = rate_ref[t : t + 1, :]
        rate_top = rate.astype(BF16).astype(F32)
        rate_low = rate - rate_top
        item = jnp.where(active, item_ref[t : t + 1, :], -1)
        step = 64

        def body(i, _):
            at = pl.ds(pl.multiple_of(i * step, step), step)
            hit = (iota((step, entries), 0) + i * step) == item
            b_one[at, :] = jnp.where(hit, 1.0, 0.0).astype(BF16)
            b_hi[at, :] = jnp.where(hit, rate_top, 0.0).astype(BF16)
            b_lo[at, :] = jnp.where(hit, rate_low, 0.0).astype(BF16)
            return 0

        lax.fori_loop(0, items // step, body, 0)

    def counts_and_ratings(t):
        pos = pos_tab[t : t + 1, :]

        def body(i, _):
            at = pl.ds(pl.multiple_of(i * RUN, RUN), RUN)
            here = (iota((RUN, entries), 0) + i * RUN).astype(F32)
            hot = onehot(here == pos)
            num[at, :] = mm(hot, b_one[...], NT)
            rat[at, :] = mm(hot, b_hi[...], NT) + mm(hot, b_lo[...], NT)
            return 0

        lax.fori_loop(0, GROUPS, body, 0)

    def split_v():
        top, low = halves(v_cur[...])
        v_hi[...] = top
        v_lo[...] = low

    load_v.wait()
    split_v()
    one_hot_items(0)

    def select_rows(t):
        mask = mask_recv[:, t, :]
        before = onehot(iota((RUN, RUN), 0) < iota((RUN, RUN), 1))
        rank = mm(mask.astype(BF16), before, NN)
        spread = onehot(iota((OWNERS * TOUCH, OWNERS), 0) // TOUCH == iota((OWNERS * TOUCH, OWNERS), 1))
        rank_rows = mm(spread, rank.astype(BF16), NN)
        mask_rows = mm(spread, mask.astype(BF16), NN)
        index = (iota((OWNERS * TOUCH, RUN), 0) % TOUCH).astype(F32)
        hit = jnp.where(rank_rows == index, mask_rows, 0.0)
        sel[t] = hit.astype(BF16)
        sel_t[t] = hit.T.astype(BF16)

    def send_rows(t):
        for group in ORDER:
            hot = sel[t, rows_of(group), :]
            rows = mm(hot, u_parts[0], NN) + mm(hot, u_parts[1], NN)
            for slot in slots_of(group):
                part = rows[(slot % SIDE) * TOUCH : (slot % SIDE + 1) * TOUCH, :]
                if slot:
                    u_send[t, slot] = part
                else:
                    u_recv[t, slot] = part
            for slot in slots_of(group):
                if slot:
                    u_copy(t, slot).start()

    def tile_rows(t):
        for group in ORDER:
            for slot in slots_of(group):
                if slot:
                    u_copy(t, slot).wait_recv()
            at = rows_of(group)
            top, low = halves(u_recv[t, group * SIDE : (group + 1) * SIDE].reshape(RUN, -1))
            ut_hi[at, :] = top
            ut_lo[at, :] = low
            v = (v_hi[...], v_lo[...])
            w = rat[at, :] - num[at, :] * mm3((top, low), v, NT)
            w_top, w_low = halves(w)
            w_hi[at, :] = w_top
            w_lo[at, :] = w_low
            grad = mm3((w_top, w_low), v, NN)
            for slot in slots_of(group):
                part = grad[(slot % SIDE) * TOUCH : (slot % SIDE + 1) * TOUCH, :]
                if slot:
                    g_send[t, slot] = part
                else:
                    g_recv[t, slot] = part
            for slot in slots_of(group):
                if slot:
                    g_copy(t, slot).start()

    def item_step(t):
        step = steps_of(t)

        def body(i, _):
            at = pl.ds(pl.multiple_of(i * RUN, RUN), RUN)
            grad = mm3((w_hi[:, at], w_lo[:, at]), (ut_hi[...], ut_lo[...]), TN)
            v_new[t, at, :] = v_cur[at, :] + step * (grad - 0.1 * v_cur[at, :])
            return 0

        lax.fori_loop(0, items // RUN, body, 0)

    def user_step(t):
        total = jnp.zeros_like(u_own[...])
        for group in ORDER:
            for slot in slots_of(group):
                if slot:
                    g_copy(t, slot).wait_recv()
            top, low = halves(g_recv[t, group * SIDE : (group + 1) * SIDE].reshape(RUN, -1))
            back = sel_t[t, :, rows_of(group)]
            total = total + mm(back, top, NN) + mm(back, low, NN)
        old = u_own[...]
        return old + steps_of(t) * (total - 0.1 * old)


    for slot in range(1, OWNERS):
        mask_copy(slot).wait_recv()
    select_rows(0)
    send_rows(0)
    counts_and_ratings(0)
    tile_rows(0)
    item_step(0)
    v_first = pltpu.make_async_remote_copy(
        src_ref=v_new.at[0], dst_ref=v_new.at[1],
        send_sem=v_ss.at[0], recv_sem=v_rs.at[0],
        device_id=(up, place), device_id_type=MESH)
    v_first.start()
    select_rows(1)
    one_hot_items(1)
    counts_and_ratings(1)
    fresh = user_step(0)
    u_own[...] = fresh
    top, low = halves(fresh)
    u_parts[0] = top
    u_parts[1] = low
    send_rows(1)
    v_first.wait()
    v_cur[...] = v_new[1]
    split_v()
    tile_rows(1)
    item_step(1)
    v_last = pltpu.make_async_remote_copy(
        src_ref=v_new.at[1], dst_ref=out_v,
        send_sem=v_ss.at[1], recv_sem=v_rs.at[1],
        device_id=(down, place), device_id_type=MESH)
    v_last.start()
    out_u[...] = user_step(1)
    for slot in range(1, OWNERS):
        mask_copy(slot).wait_send()
        for t in range(subs):
            u_copy(t, slot).wait_send()
            g_copy(t, slot).wait_send()
    v_last.wait()


def on_device(n_rows, user_factors, item_factors, ratings, user_offsets, item_offsets, counts):
    users, rank = user_factors.shape
    items = item_factors.shape[0]
    subs, entries = ratings.shape
    picked = OWNERS * TOUCH
    vmem = pl.BlockSpec(memory_space=pltpu.VMEM)
    hbm = pl.BlockSpec(memory_space=pl.ANY)
    dma = pltpu.SemaphoreType.DMA
    return pl.pallas_call(
        functools.partial(kernel, n_rows),
        out_shape=(
            jax.ShapeDtypeStruct((users, rank), F32),
            jax.ShapeDtypeStruct((items, rank), F32),
        ),
        in_specs=[hbm, hbm, vmem, vmem, vmem, vmem],
        out_specs=(vmem, vmem),
        scratch_shapes=[
            pltpu.VMEM((users, rank), F32),
            pltpu.VMEM((items, rank), F32),
            pltpu.VMEM((subs, items, rank), F32),
            pltpu.VMEM((items, rank), BF16),
            pltpu.VMEM((items, rank), BF16),
            pltpu.VMEM((OWNERS, 8, RUN), F32),
            pltpu.VMEM((OWNERS, 8, RUN), F32),
            pltpu.VMEM((8, 128), F32),
            pltpu.VMEM((8, entries), F32),
            pltpu.VMEM((subs, picked, RUN), BF16),
            pltpu.VMEM((subs, RUN, picked), BF16),
            pltpu.VMEM((items, entries), BF16),
            pltpu.VMEM((items, entries), BF16),
            pltpu.VMEM((items, entries), BF16),
            pltpu.VMEM((picked, items), F32),
            pltpu.VMEM((picked, items), F32),
            pltpu.VMEM((picked, rank), BF16),
            pltpu.VMEM((picked, rank), BF16),
            pltpu.VMEM((picked, items), BF16),
            pltpu.VMEM((picked, items), BF16),
            pltpu.VMEM((subs, OWNERS, TOUCH, rank), F32),
            pltpu.VMEM((subs, OWNERS, TOUCH, rank), F32),
            pltpu.VMEM((subs, OWNERS, TOUCH, rank), F32),
            pltpu.VMEM((subs, OWNERS, TOUCH, rank), F32),
            pltpu.VMEM((2, users, rank), BF16),
            dma((2,)),
            dma((OWNERS,)),
            dma((OWNERS,)),
            dma((subs, OWNERS)),
            dma((subs, OWNERS)),
            dma((subs, OWNERS)),
            dma((subs, OWNERS)),
            dma((2,)),
            dma((2,)),
        ],
        compiler_params=pltpu.CompilerParams(
            collective_id=0, has_side_effects=True, vmem_limit_bytes=56 * 1024 * 1024
        ),
        name="sgd",
    )(user_factors, item_factors, ratings, user_offsets, item_offsets, counts)


def solution(mesh):
    shard = P(("rows", "strata"), None)
    split = P(None, ("rows", "strata"))
    return jax.shard_map(
        functools.partial(on_device, mesh.shape["rows"]),
        mesh=mesh,
        in_specs=(shard, shard, split, split, split, split),
        out_specs=(shard, shard),
        check_vma=False,
    )
```

```python
import functools

import jax
import jax.numpy as jnp
from jax import lax
from jax.experimental import pallas as pl
from jax.experimental.pallas import tpu as pltpu
from jax.sharding import PartitionSpec as P

MESH = pl.DeviceIdType.MESH
F32 = jnp.float32
BF16 = jnp.bfloat16

SIDE = 4
OWNERS = SIDE * SIDE
RUN = 128
TOUCH = 32
GROUPS = SIDE
STEPS = (0, 1, 3, 2)

NN = (((1,), (0,)), ((), ()))
NT = (((1,), (1,)), ((), ()))
TN = (((0,), (0,)), ((), ()))


def mm(a, b, dims):
    return lax.dot_general(a, b, dims, preferred_element_type=F32)


def halves(value):
    top = value.astype(BF16)
    return top, (value - top.astype(F32)).astype(BF16)


def mm3(a, b, dims):
    return mm(a[0], b[0], dims) + mm(a[0], b[1], dims) + mm(a[1], b[0], dims)


def iota(shape, dim):
    return lax.broadcasted_iota(jnp.int32, shape, dim)


def onehot(test):
    return jnp.where(test, 1.0, 0.0).astype(BF16)


def steps_of(sub_epoch):
    return 0.04 / (1.0 + 0.5 * sub_epoch)


def kernel(
    n_rows,
    u_hbm, v_hbm, rate_ref, user_ref, item_ref, count_ref,
    out_u, out_v,
    u_own, v_cur, v_in, v_new, v_hi, v_lo,
    mask_send, mask_recv, rank_tab, pos_tab,
    sel, sel_t,
    b_one, b_hi, b_lo, num, rat,
    ut_hi, ut_lo, w_hi, w_lo,
    u_send, u_recv, g_send, g_recv, u_parts,
    load_sem, mask_ss, mask_rs, u_ss, u_rs, g_ss, g_rs, v_ss, v_rs,
):
    row = lax.axis_index("rows")
    place = lax.axis_index("strata")
    y, x = place // SIDE, place % SIDE
    up, down = (row + 1) % n_rows, (row + n_rows - 1) % n_rows
    items = v_cur.shape[0]
    entries = rate_ref.shape[1]
    subs = rate_ref.shape[0]

    def away(slot, sign):
        dy, dx = STEPS[slot // SIDE], slot % SIDE
        return ((y + sign * dy + SIDE) % SIDE) * SIDE + (x + sign * dx + SIDE) % SIDE

    def tile_of(slot):
        return (row, away(slot, 1))

    def owner_of(slot):
        return (row, away(slot, -1))

    barrier = pltpu.get_barrier_semaphore()
    for slot in range(1, OWNERS):
        pl.semaphore_signal(barrier, inc=1, device_id=tile_of(slot), device_id_type=MESH)
    for other in (up, down):
        pl.semaphore_signal(barrier, inc=1, device_id=(other, place), device_id_type=MESH)

    load_u = pltpu.make_async_copy(u_hbm, u_own, load_sem.at[0])
    load_v = pltpu.make_async_copy(v_hbm, v_cur, load_sem.at[1])
    load_u.start()
    load_v.start()

    def slot_and_run(t):
        user = user_ref[t : t + 1, :]
        owner = user >> 7
        dy = (y + SIDE - (owner >> 2)) & 3
        dx = (x + SIDE - (owner & 3)) & 3
        return (dy ^ (dy >> 1)) * SIDE + dx, user & (RUN - 1)

    for t in range(subs):
        slot_e, low_e = slot_and_run(t)
        hot_slot = onehot(iota((OWNERS, entries), 0) == slot_e)
        hot_low = onehot(iota((RUN, entries), 0) == low_e)
        named = jnp.where(mm(hot_slot, hot_low, NT) > 0.5, 1.0, 0.0)
        mask_send[:, t, :] = named
        before = onehot(iota((RUN, RUN), 0) < iota((RUN, RUN), 1))
        rank = mm(named.astype(BF16), before, NN)
        each = mm(rank.astype(BF16), hot_low, NN)
        rank_e = jnp.sum(jnp.where(iota((OWNERS, entries), 0) == slot_e, each, 0.0), axis=0, keepdims=True)
        pos_tab[t : t + 1, :] = slot_e.astype(F32) * float(TOUCH) + rank_e

    pl.semaphore_wait(barrier, OWNERS + 1)

    def mask_copy(slot):
        return pltpu.make_async_remote_copy(
            src_ref=mask_send.at[slot], dst_ref=mask_recv.at[slot],
            send_sem=mask_ss, recv_sem=mask_rs,
            device_id=owner_of(slot), device_id_type=MESH)

    cut = u_own.shape[1] // 2
    WHOLE = slice(0, 2 * cut)
    HALVES = (slice(0, cut), slice(cut, 2 * cut))

    def parts_of(split):
        return HALVES if split else (WHOLE,)

    def u_copy(t, slot, cols):
        part = 1 if cols.start else 0
        return pltpu.make_async_remote_copy(
            src_ref=u_send.at[t, slot, :, cols], dst_ref=u_recv.at[t, slot, :, cols],
            send_sem=u_ss, recv_sem=u_rs.at[t, part, slot // SIDE],
            device_id=tile_of(slot), device_id_type=MESH)

    def g_copy(t, slot, cols):
        part = 1 if cols.start else 0
        return pltpu.make_async_remote_copy(
            src_ref=g_send.at[t, slot, :, cols], dst_ref=g_recv.at[t, slot, :, cols],
            send_sem=g_ss, recv_sem=g_rs.at[t, part, slot // SIDE],
            device_id=owner_of(slot), device_id_type=MESH)

    def arrived(recv, sems, t, group, cols):
        first = max(1, group * SIDE)
        part = recv.at[t, first : (group + 1) * SIDE, :, cols]
        sem = sems.at[t, 1 if cols.start else 0, group]
        pltpu.make_async_copy(part, part, sem).wait()

    def slots_of(group):
        return range(group * SIDE, (group + 1) * SIDE)

    def rows_of(group):
        return slice(group * RUN, (group + 1) * RUN)

    for group in range(GROUPS):
        for slot in slots_of(group):
            if slot:
                mask_copy(slot).start()
    mask_recv[0] = mask_send[0]

    load_u.wait()
    top, low = halves(u_own[...])
    u_parts[0] = top
    u_parts[1] = low

    def one_hot_items(t):
        active = iota((1, entries), 1) < count_ref[0:1, t : t + 1]
        rate = rate_ref[t : t + 1, :]
        rate_top = rate.astype(BF16).astype(F32)
        rate_low = rate - rate_top
        item = jnp.where(active, item_ref[t : t + 1, :], -1)
        step = 64

        def body(i, _):
            at = pl.ds(pl.multiple_of(i * step, step), step)
            hit = (iota((step, entries), 0) + i * step) == item
            b_one[at, :] = jnp.where(hit, 1.0, 0.0).astype(BF16)
            b_hi[at, :] = jnp.where(hit, rate_top, 0.0).astype(BF16)
            b_lo[at, :] = jnp.where(hit, rate_low, 0.0).astype(BF16)
            return 0

        lax.fori_loop(0, items // step, body, 0)

    def counts_and_ratings(t):
        pos = pos_tab[t : t + 1, :]

        def body(i, _):
            at = pl.ds(pl.multiple_of(i * RUN, RUN), RUN)
            here = (iota((RUN, entries), 0) + i * RUN).astype(F32)
            hot = onehot(here == pos)
            num[t, at, :] = mm(hot, b_one[...], NT)
            rat[t, at, :] = mm(hot, b_hi[...], NT) + mm(hot, b_lo[...], NT)
            return 0

        lax.fori_loop(0, GROUPS, body, 0)

    def split_v():
        top, low = halves(v_cur[...])
        v_hi[...] = top
        v_lo[...] = low

    load_v.wait()
    split_v()

    def select_rows(t):
        mask = mask_recv[:, t, :]
        before = onehot(iota((RUN, RUN), 0) < iota((RUN, RUN), 1))
        rank = mm(mask.astype(BF16), before, NN)
        spread = onehot(iota((OWNERS * TOUCH, OWNERS), 0) // TOUCH == iota((OWNERS * TOUCH, OWNERS), 1))
        rank_rows = mm(spread, rank.astype(BF16), NN)
        mask_rows = mm(spread, mask.astype(BF16), NN)
        index = (iota((OWNERS * TOUCH, RUN), 0) % TOUCH).astype(F32)
        hit = jnp.where(rank_rows == index, mask_rows, 0.0)
        sel[t] = hit.astype(BF16)
        sel_t[t] = hit.T.astype(BF16)

    def send_rows(t, cols):
        for group in range(GROUPS):
            hot = sel[t, rows_of(group), :]
            rows = mm(hot, u_parts[0, :, cols], NN) + mm(hot, u_parts[1, :, cols], NN)
            for slot in slots_of(group):
                part = rows[(slot % SIDE) * TOUCH : (slot % SIDE + 1) * TOUCH, :]
                if slot:
                    u_send[t, slot, :, cols] = part
                else:
                    u_recv[t, slot, :, cols] = part
            for slot in slots_of(group):
                if slot:
                    u_copy(t, slot, cols).start()

    def tile_rows(t, u_split, g_split):
        held = []
        for group in range(GROUPS):
            if group == GROUPS - 1:
                item_begin(t)
            for cols in parts_of(u_split):
                arrived(u_recv, u_rs, t, group, cols)
            if t + 1 == subs and group == GROUPS - 1:
                for slot, cols in held:
                    g_copy(t, slot, cols).start()
                held = []
            at = rows_of(group)
            top, low = halves(u_recv[t, group * SIDE : (group + 1) * SIDE].reshape(RUN, -1))
            ut_hi[at, :] = top
            ut_lo[at, :] = low
            v = (v_hi[...], v_lo[...])
            w = rat[t, at, :] - num[t, at, :] * mm3((top, low), v, NT)
            w_top, w_low = halves(w)
            w_hi[at, :] = w_top
            w_lo[at, :] = w_low
            grad = mm3((w_top, w_low), v, NN)
            for slot in slots_of(group):
                part = grad[(slot % SIDE) * TOUCH : (slot % SIDE + 1) * TOUCH, :]
                if slot:
                    g_send[t, slot] = part
                else:
                    g_recv[t, slot] = part
            last_group = group == GROUPS - 1
            for part, cols in enumerate(parts_of(g_split)):
                for slot in slots_of(group):
                    if slot:
                        if not last_group and (part or t + 1 == subs):
                            held.append((slot, cols))
                        elif not part:
                            g_copy(t, slot, cols).start()
                        else:
                            held.append((slot, cols))
        for slot, cols in held:
            g_copy(t, slot, cols).start()

    def user_step(t, cols):
        old = u_own[:, cols]
        total = jnp.zeros_like(old)
        for group in range(GROUPS):
            arrived(g_recv, g_rs, t, group, cols)
            top, low = halves(g_recv[t, group * SIDE : (group + 1) * SIDE, :, cols].reshape(RUN, -1))
            back = sel_t[t, :, rows_of(group)]
            total = total + mm(back, top, NN) + mm(back, low, NN)
        u_own[:, cols] = old + steps_of(t) * (total - 0.1 * old)

    def update_half(t, cols):
        user_step(t, cols)
        top, low = halves(u_own[:, cols])
        u_parts[0, :, cols] = top
        u_parts[1, :, cols] = low
        send_rows(t + 1, cols)

    def v_copy(t, chunk):
        at = pl.ds(chunk * RUN, RUN)
        dst = out_v if t + 1 == subs else v_in
        return pltpu.make_async_remote_copy(
            src_ref=v_new.at[t, at], dst_ref=dst.at[at],
            send_sem=v_ss, recv_sem=v_rs.at[t],
            device_id=(down if t + 1 == subs else up, place), device_id_type=MESH)

    def item_grad(t, first, last, chunk):
        at = slice(chunk * RUN, (chunk + 1) * RUN)
        rows = slice(first * RUN, last * RUN)
        return mm3((w_hi[rows, at], w_lo[rows, at]), (ut_hi[rows, :], ut_lo[rows, :]), TN)

    def item_begin(t):
        for chunk in range(items // RUN):
            v_new[t, chunk * RUN : (chunk + 1) * RUN, :] = item_grad(t, 0, GROUPS - 1, chunk)

    def item_step(t):
        step = steps_of(t)
        for chunk in range(items // RUN):
            at = slice(chunk * RUN, (chunk + 1) * RUN)
            grad = v_new[t, at, :] + item_grad(t, GROUPS - 1, GROUPS, chunk)
            v_new[t, at, :] = v_cur[at, :] + step * (grad - 0.1 * v_cur[at, :])
            v_copy(t, chunk).start()

    one_hot_items(0)
    counts_and_ratings(0)
    def wait_masks():
        pltpu.make_async_copy(mask_recv.at[1:OWNERS], mask_recv.at[1:OWNERS], mask_rs).wait()

    wait_masks()
    select_rows(0)
    send_rows(0, WHOLE)
    select_rows(1)
    one_hot_items(1)
    counts_and_ratings(1)
    tile_rows(0, False, False)
    item_step(0)
    update_half(0, WHOLE)

    def wait_v():
        pltpu.make_async_copy(v_in, v_in, v_rs.at[0]).wait()

    wait_v()
    v_cur[...] = v_in[...]
    split_v()
    tile_rows(1, False, False)
    item_step(1)
    user_step(1, WHOLE)
    put_u = pltpu.make_async_copy(u_own, out_u, load_sem.at[0])
    put_u.start()
    def finish():
        for sent, sem in ((mask_send.at[1:OWNERS], mask_ss), (u_send.at[:, 1:OWNERS], u_ss), (g_send.at[:, 1:OWNERS], g_ss)):
            pltpu.make_async_copy(sent, sent, sem).wait()
        pltpu.make_async_copy(v_new, v_new, v_ss).wait()
        pltpu.make_async_copy(out_v, out_v, v_rs.at[1]).wait()
        put_u.wait()

    finish()


def on_device(n_rows, user_factors, item_factors, ratings, user_offsets, item_offsets, counts):
    users, rank = user_factors.shape
    items = item_factors.shape[0]
    subs, entries = ratings.shape
    picked = OWNERS * TOUCH
    vmem = pl.BlockSpec(memory_space=pltpu.VMEM)
    hbm = pl.BlockSpec(memory_space=pl.ANY)
    dma = pltpu.SemaphoreType.DMA
    return pl.pallas_call(
        functools.partial(kernel, n_rows),
        out_shape=(
            pltpu.VMEM((users, rank), F32),
            pltpu.VMEM((items, rank), F32),
        ),
        in_specs=[hbm, hbm, vmem, vmem, vmem, vmem],
        out_specs=(hbm, hbm),
        scratch_shapes=[
            pltpu.VMEM((users, rank), F32),
            pltpu.VMEM((items, rank), F32),
            pltpu.VMEM((items, rank), F32),
            pltpu.VMEM((subs, items, rank), F32),
            pltpu.VMEM((items, rank), BF16),
            pltpu.VMEM((items, rank), BF16),
            pltpu.VMEM((OWNERS, 8, RUN), F32),
            pltpu.VMEM((OWNERS, 8, RUN), F32),
            pltpu.VMEM((8, 128), F32),
            pltpu.VMEM((8, entries), F32),
            pltpu.VMEM((subs, picked, RUN), BF16),
            pltpu.VMEM((subs, RUN, picked), BF16),
            pltpu.VMEM((items, entries), BF16),
            pltpu.VMEM((items, entries), BF16),
            pltpu.VMEM((items, entries), BF16),
            pltpu.VMEM((subs, picked, items), F32),
            pltpu.VMEM((subs, picked, items), F32),
            pltpu.VMEM((picked, rank), BF16),
            pltpu.VMEM((picked, rank), BF16),
            pltpu.VMEM((picked, items), BF16),
            pltpu.VMEM((picked, items), BF16),
            pltpu.VMEM((subs, OWNERS, TOUCH, rank), F32),
            pltpu.VMEM((subs, OWNERS, TOUCH, rank), F32),
            pltpu.VMEM((subs, OWNERS, TOUCH, rank), F32),
            pltpu.VMEM((subs, OWNERS, TOUCH, rank), F32),
            pltpu.VMEM((2, users, rank), BF16),
            dma((2,)),
            dma,
            dma,
            dma,
            dma((subs, 2, GROUPS)),
            dma,
            dma((subs, 2, GROUPS)),
            dma,
            dma((subs,)),
        ],
        compiler_params=pltpu.CompilerParams(
            collective_id=0, has_side_effects=True, vmem_limit_bytes=56 * 1024 * 1024
        ),
        name="sgd",
    )(user_factors, item_factors, ratings, user_offsets, item_offsets, counts.T)


def solution(mesh):
    shard = P(("rows", "strata"), None)
    split = P(None, ("rows", "strata"))
    return jax.shard_map(
        functools.partial(on_device, mesh.shape["rows"]),
        mesh=mesh,
        in_specs=(shard, shard, split, split, split, split),
        out_specs=(shard, shard),
        check_vma=False,
    )
```

```python
import functools

import jax
import jax.numpy as jnp
from jax import lax
from jax.experimental import pallas as pl
from jax.experimental.pallas import tpu as pltpu
from jax.sharding import PartitionSpec as P

MESH = pl.DeviceIdType.MESH
F32 = jnp.float32
BF16 = jnp.bfloat16

SIDE = 4
OWNERS = SIDE * SIDE
RUN = 128
TOUCH = 32
GROUPS = SIDE
STEPS = (0, 1, 3, 2)

NN = (((1,), (0,)), ((), ()))
NT = (((1,), (1,)), ((), ()))
TN = (((0,), (0,)), ((), ()))


def mm(a, b, dims):
    return lax.dot_general(a, b, dims, preferred_element_type=F32)


def halves(value):
    top = value.astype(BF16)
    return top, (value - top.astype(F32)).astype(BF16)


def mm3(a, b, dims):
    return mm(a[0], b[0], dims) + mm(a[0], b[1], dims) + mm(a[1], b[0], dims)


def iota(shape, dim):
    return lax.broadcasted_iota(jnp.int32, shape, dim)


def onehot(test):
    return jnp.where(test, 1.0, 0.0).astype(BF16)


def steps_of(sub_epoch):
    return 0.04 / (1.0 + 0.5 * sub_epoch)


def kernel(
    n_rows,
    u_hbm, v_hbm, rate_ref, user_ref, item_ref, count_ref,
    out_u, out_v,
    u_own, v_cur, v_in, v_new, v_hi, v_lo,
    mask_send, mask_recv, rank_tab, pos_tab,
    sel, sel_t,
    b_one, b_hi, b_lo, num, rat,
    ut_hi, ut_lo, w_hi, w_lo,
    u_send, u_recv, g_send, g_recv, u_parts,
    relay_mask, dense, relay_send,
    pack_send, pack_recv, away_rows, own_hi, own_lo,
    pack_ss, pack_rs, away_ss, away_rs,
    dense_ss, relay_ss, relay_ms, relay_mrs, dense_rs, relay_rs,
    load_sem, mask_ss, mask_rs, u_ss, u_rs, g_ss, g_rs, v_ss, v_rs,
):
    row = lax.axis_index("rows")
    place = lax.axis_index("strata")
    y, x = place // SIDE, place % SIDE
    up, down = (row + 1) % n_rows, (row + n_rows - 1) % n_rows
    items = v_cur.shape[0]
    entries = rate_ref.shape[1]
    subs = rate_ref.shape[0]

    def away(slot, sign):
        dy, dx = STEPS[slot // SIDE], slot % SIDE
        return ((y + sign * dy + SIDE) % SIDE) * SIDE + (x + sign * dx + SIDE) % SIDE

    def tile_of(slot):
        return (row, away(slot, 1))

    def owner_of(slot):
        return (row, away(slot, -1))

    barrier = pltpu.get_barrier_semaphore()
    for slot in range(1, OWNERS):
        pl.semaphore_signal(barrier, inc=1, device_id=tile_of(slot), device_id_type=MESH)
    for other in (up, down):
        pl.semaphore_signal(barrier, inc=1, device_id=(other, place), device_id_type=MESH)

    load_u = pltpu.make_async_copy(u_hbm, u_own, load_sem.at[0])
    load_v = pltpu.make_async_copy(v_hbm, v_cur, load_sem.at[1])
    load_u.start()
    load_v.start()

    def slot_and_run(t):
        user = user_ref[t : t + 1, :]
        owner = user >> 7
        dy = (y + SIDE - (owner >> 2)) & 3
        dx = (x + SIDE - (owner & 3)) & 3
        return (dy ^ (dy >> 1)) * SIDE + dx, user & (RUN - 1)

    for t in range(subs):
        slot_e, low_e = slot_and_run(t)
        hot_slot = onehot(iota((OWNERS, entries), 0) == slot_e)
        hot_low = onehot(iota((RUN, entries), 0) == low_e)
        named = jnp.where(mm(hot_slot, hot_low, NT) > 0.5, 1.0, 0.0)
        mask_send[:, :, t, :] = named.reshape(GROUPS, SIDE, RUN)
        before = onehot(iota((RUN, RUN), 0) < iota((RUN, RUN), 1))
        rank = mm(named.astype(BF16), before, NN)
        each = mm(rank.astype(BF16), hot_low, NN)
        rank_e = jnp.sum(jnp.where(iota((OWNERS, entries), 0) == slot_e, each, 0.0), axis=0, keepdims=True)
        pos_tab[t : t + 1, :] = slot_e.astype(F32) * float(TOUCH) + rank_e

    pack_send[0:1, :] = pos_tab[subs - 1 : subs, :]
    pack_send[1:2, :] = jnp.where(
        iota((1, entries), 1) < count_ref[0:1, subs - 1 : subs], item_ref[subs - 1 : subs, :], -1
    ).astype(F32)
    pack_send[2:3, :] = rate_ref[subs - 1 : subs, :]
    pl.semaphore_wait(barrier, OWNERS + 1)

    def mask_copy(slot):
        return pltpu.make_async_remote_copy(
            src_ref=mask_send.at[slot // SIDE, slot % SIDE], dst_ref=mask_recv.at[slot],
            send_sem=mask_ss, recv_sem=mask_rs,
            device_id=owner_of(slot), device_id_type=MESH)

    cut = u_own.shape[1] // 2
    HALVES = (slice(0, cut), slice(cut, 2 * cut))

    def u_copy(slot):
        return pltpu.make_async_remote_copy(
            src_ref=u_send.at[slot], dst_ref=u_recv.at[1, slot // SIDE, slot % SIDE],
            send_sem=u_ss, recv_sem=u_rs.at[slot // SIDE],
            device_id=tile_of(slot), device_id_type=MESH)

    def g_copy(t, slot):
        return pltpu.make_async_remote_copy(
            src_ref=g_send.at[t, slot], dst_ref=g_recv.at[t, slot],
            send_sem=g_ss, recv_sem=g_rs.at[t, slot // SIDE],
            device_id=owner_of(slot), device_id_type=MESH)

    def rows_in(t, group):
        if t:
            all_in(u_recv.at[t, group, (1 if group == 0 else 0) :], u_rs.at[group])
            return
        if group == 0:
            for step in range(1, SIDE):
                all_in(u_recv.at[0, :, step, :, HALVES[1]], relay_rs.at[1, step])
        else:
            all_in(u_recv.at[0, group, :, :, HALVES[0]], relay_rs.at[0, group])

    def grads_in(t, group):
        first = max(1, group * SIDE)
        all_in(g_recv.at[t, first : (group + 1) * SIDE], g_rs.at[t, group])

    def slots_of(group):
        return range(group * SIDE, (group + 1) * SIDE)

    def rows_of(group):
        return slice(group * RUN, (group + 1) * RUN)

    def named_items(t):
        active = iota((1, entries), 1) < count_ref[0:1, t : t + 1]
        return jnp.where(active, item_ref[t : t + 1, :], -1).astype(F32)

    def one_hot_items(t):
        if t < subs:
            rate, item = rate_ref[t : t + 1, :], named_items(t)
        else:
            rate, item = pack_recv[2:3, :], pack_recv[1:2, :]
        rate_top = rate.astype(BF16).astype(F32)
        rate_low = rate - rate_top
        step = 64

        def body(i, _):
            at = pl.ds(pl.multiple_of(i * step, step), step)
            hit = (iota((step, entries), 0) + i * step).astype(F32) == item
            b_one[at, :] = jnp.where(hit, 1.0, 0.0).astype(BF16)
            b_hi[at, :] = jnp.where(hit, rate_top, 0.0).astype(BF16)
            b_lo[at, :] = jnp.where(hit, rate_low, 0.0).astype(BF16)
            return 0

        lax.fori_loop(0, items // step, body, 0)

    def counts_and_ratings(t):
        pos = pos_tab[t : t + 1, :] if t < subs else pack_recv[0:1, :]

        def body(i, _):
            at = pl.ds(pl.multiple_of(i * RUN, RUN), RUN)
            here = (iota((RUN, entries), 0) + i * RUN).astype(F32)
            hot = onehot(here == pos)
            num[t, at, :] = mm(hot, b_one[...], NT)
            rat[t, at, :] = mm(hot, b_hi[...], NT) + mm(hot, b_lo[...], NT)
            return 0

        lax.fori_loop(0, GROUPS, body, 0)

    def split_v():
        top, low = halves(v_cur[...])
        v_hi[...] = top
        v_lo[...] = low


    def relay_place(hop, step, sign):
        dy, dx = (0, step) if hop == 0 else (STEPS[step], 0)
        return (row, ((y + sign * dy + SIDE) % SIDE) * SIDE + (x + sign * dx + SIDE) % SIDE)

    def dense_copy(hop, step):
        return pltpu.make_async_remote_copy(
            src_ref=u_own.at[:, HALVES[hop]], dst_ref=dense.at[hop, step],
            send_sem=dense_ss, recv_sem=dense_rs.at[hop],
            device_id=relay_place(hop, step, 1), device_id_type=MESH)

    def relay_mask_copy(hop, step):
        src = mask_send.at[step] if hop == 0 else mask_send.at[:, step]
        return pltpu.make_async_remote_copy(
            src_ref=src, dst_ref=relay_mask.at[hop, step],
            send_sem=relay_ms, recv_sem=relay_mrs.at[hop],
            device_id=relay_place(1 - hop, step, -1), device_id_type=MESH)

    def relay_copy(hop, step):
        cols = HALVES[hop]
        dst = u_recv.at[0, step, :, :, cols] if hop == 0 else u_recv.at[0, :, step, :, cols]
        return pltpu.make_async_remote_copy(
            src_ref=relay_send.at[hop, step], dst_ref=dst,
            send_sem=relay_ss, recv_sem=relay_rs.at[hop, step],
            device_id=relay_place(1 - hop, step, 1), device_id_type=MESH)

    def all_in(part, sem):
        pltpu.make_async_copy(part, part, sem).wait()

    def relay_out(hop):
        all_in(relay_mask.at[hop, 1:SIDE], relay_mrs.at[hop])
        if hop == 0:
            relay_mask[hop, 0] = mask_send[0]
        else:
            relay_mask[hop, 0] = mask_send[:, 0]
        mask = relay_mask[hop, :, :, 0, :].reshape(OWNERS, RUN)
        before = onehot(iota((RUN, RUN), 0) < iota((RUN, RUN), 1))
        rank = mm(mask.astype(BF16), before, NN)
        line = iota((OWNERS * TOUCH, OWNERS), 0)
        spread = onehot((line // TOUCH % SIDE) * SIDE + line // RUN == iota((OWNERS * TOUCH, OWNERS), 1))
        rank_rows = mm(spread, rank.astype(BF16), NN)
        mask_rows = mm(spread, mask.astype(BF16), NN)
        index = (iota((OWNERS * TOUCH, RUN), 0) % TOUCH).astype(F32)
        hit = jnp.where(rank_rows == index, mask_rows, 0.0).astype(BF16)
        all_in(dense.at[hop, 1:SIDE], dense_rs.at[hop])
        for step in range(SIDE):
            held = u_own[:, HALVES[hop]] if step == 0 else dense[hop, step]
            top, low = halves(held)
            hot = hit[step * RUN : (step + 1) * RUN, :]
            rows = mm(hot, top, NN) + mm(hot, low, NN)
            for to in range(SIDE):
                part = rows[to * TOUCH : (to + 1) * TOUCH, :]
                if to:
                    relay_send[hop, to, step] = part
                elif hop == 0:
                    u_recv[0, 0, step, :, HALVES[0]] = part
                else:
                    u_recv[0, step, 0, :, HALVES[1]] = part
        for to in range(1, SIDE):
            relay_copy(hop, to).start()

    def select_rows(t):
        mask = mask_recv[:, t, :]
        before = onehot(iota((RUN, RUN), 0) < iota((RUN, RUN), 1))
        rank = mm(mask.astype(BF16), before, NN)
        spread = onehot(iota((OWNERS * TOUCH, OWNERS), 0) // TOUCH == iota((OWNERS * TOUCH, OWNERS), 1))
        rank_rows = mm(spread, rank.astype(BF16), NN)
        mask_rows = mm(spread, mask.astype(BF16), NN)
        index = (iota((OWNERS * TOUCH, RUN), 0) % TOUCH).astype(F32)
        hit = jnp.where(rank_rows == index, mask_rows, 0.0)
        if t:
            sel[...] = hit.astype(BF16)
        sel_t[t] = hit.T.astype(BF16)

    def send_rows():
        for group in range(GROUPS):
            hot = sel[rows_of(group), :]
            rows = mm(hot, u_parts[0], NN) + mm(hot, u_parts[1], NN)
            for slot in slots_of(group):
                part = rows[(slot % SIDE) * TOUCH : (slot % SIDE + 1) * TOUCH, :]
                if slot:
                    u_send[slot] = part
                else:
                    u_recv[1, 0, 0] = part
            for slot in slots_of(group):
                if slot:
                    u_copy(slot).start()

    def away_copy(group):
        return pltpu.make_async_remote_copy(
            src_ref=u_recv.at[subs - 1, group], dst_ref=away_rows.at[group],
            send_sem=away_ss, recv_sem=away_rs.at[group],
            device_id=(down, place), device_id_type=MESH)

    def away_items():
        t = subs - 1
        own = (own_hi[...], own_lo[...])
        for group in range(GROUPS):
            all_in(away_rows.at[group], away_rs.at[group])
            at = rows_of(group)
            top, low = halves(away_rows[group].reshape(RUN, -1))
            ut_hi[at, :] = top
            ut_lo[at, :] = low
            w_top, w_low = halves(rat[subs, at, :] - num[subs, at, :] * mm3((top, low), own, NT))
            w_hi[at, :] = w_top
            w_lo[at, :] = w_low
        for chunk in range(items // RUN):
            at = slice(chunk * RUN, (chunk + 1) * RUN)
            old = v_new[at, :]
            v_cur[at, :] = old + steps_of(t) * (item_grad(0, GROUPS, chunk) - 0.1 * old)

    def tile_rows(t):
        held = []
        for group in range(GROUPS):
            if group == GROUPS - 1 and t + 1 < subs:
                item_begin()
            rows_in(t, group)
            if t + 1 == subs:
                away_copy(group).start()
            if group == GROUPS - 1:
                for slot in held:
                    g_copy(t, slot).start()
            at = rows_of(group)
            top, low = halves(u_recv[t, group].reshape(RUN, -1))
            v = (v_hi[...], v_lo[...])
            w = rat[t, at, :] - num[t, at, :] * mm3((top, low), v, NT)
            w_top, w_low = halves(w)
            if t + 1 < subs:
                ut_hi[at, :] = top
                ut_lo[at, :] = low
                w_hi[at, :] = w_top
                w_lo[at, :] = w_low
            grad = mm3((w_top, w_low), v, NN)
            for slot in slots_of(group):
                part = grad[(slot % SIDE) * TOUCH : (slot % SIDE + 1) * TOUCH, :]
                if slot:
                    g_send[t, slot] = part
                else:
                    g_recv[t, slot] = part
            for slot in slots_of(group):
                if slot:
                    if False:
                        held.append(slot)
                    else:
                        g_copy(t, slot).start()

    def user_step(t):
        old = u_own[...]
        total = jnp.zeros_like(old)
        for group in range(GROUPS):
            grads_in(t, group)
            top, low = halves(g_recv[t, group * SIDE : (group + 1) * SIDE].reshape(RUN, -1))
            back = sel_t[t, :, rows_of(group)]
            total = total + mm(back, top, NN) + mm(back, low, NN)
        u_own[...] = old + steps_of(t) * (total - 0.1 * old)

    def update_half():
        all_in(dense.at[:, 1:SIDE], dense_ss)
        user_step(0)
        top, low = halves(u_own[...])
        u_parts[0] = top
        u_parts[1] = low
        send_rows()

    def v_copy(chunk):
        at = pl.ds(chunk * RUN, RUN)
        return pltpu.make_async_remote_copy(
            src_ref=v_new.at[at], dst_ref=v_in.at[at],
            send_sem=v_ss, recv_sem=v_rs,
            device_id=(up, place), device_id_type=MESH)

    def item_grad(first, last, chunk):
        at = slice(chunk * RUN, (chunk + 1) * RUN)
        rows = slice(first * RUN, last * RUN)
        return mm3((w_hi[rows, at], w_lo[rows, at]), (ut_hi[rows, :], ut_lo[rows, :]), TN)

    def item_begin():
        for chunk in range(items // RUN):
            v_new[chunk * RUN : (chunk + 1) * RUN, :] = item_grad(0, GROUPS - 1, chunk)

    def item_step_0():
        step = steps_of(0)
        for chunk in range(items // RUN):
            at = slice(chunk * RUN, (chunk + 1) * RUN)
            grad = v_new[at, :] + item_grad(GROUPS - 1, GROUPS, chunk)
            fresh = v_cur[at, :] + step * (grad - 0.1 * v_cur[at, :])
            v_new[at, :] = fresh
            v_copy(chunk).start()
            top, low = halves(fresh)
            own_hi[at, :] = top
            own_lo[at, :] = low

    load_u.wait()
    for step in range(1, SIDE):
        for hop in (1, 0):
            relay_mask_copy(hop, step).start()
    for step in (1, 3, 2):
        for hop in (1, 0):
            dense_copy(hop, step if hop == 0 else (0, 1, 3, 2)[step]).start()
    for slot in range(1, OWNERS):
        mask_copy(slot).start()
    pack_copy = pltpu.make_async_remote_copy(
        src_ref=pack_send, dst_ref=pack_recv, send_sem=pack_ss, recv_sem=pack_rs,
        device_id=(down, place), device_id_type=MESH)
    pack_copy.start()
    mask_recv[0] = mask_send[0, 0]

    load_v.wait()
    split_v()
    one_hot_items(0)
    counts_and_ratings(0)
    relay_out(1)
    relay_out(0)

    def wait_masks():
        all_in(mask_recv.at[1:OWNERS], mask_rs)

    tile_rows(0)
    item_step_0()
    wait_masks()
    select_rows(0)
    select_rows(1)
    one_hot_items(1)
    counts_and_ratings(1)
    update_half()

    def wait_v():
        all_in(v_in, v_rs)

    all_in(pack_recv, pack_rs)
    one_hot_items(2)
    counts_and_ratings(2)
    wait_v()
    top, low = halves(v_in[...])
    v_hi[...] = top
    v_lo[...] = low
    tile_rows(1)
    away_items()
    put_v = pltpu.make_async_copy(v_cur, out_v, load_sem.at[1])
    put_v.start()
    user_step(1)
    put_u = pltpu.make_async_copy(u_own, out_u, load_sem.at[0])
    put_u.start()

    def finish():
        all_in(mask_recv.at[1:OWNERS], mask_ss)
        all_in(relay_mask.at[:, 1:SIDE], relay_ms)
        all_in(u_send.at[1:OWNERS], u_ss)
        all_in(g_send.at[:, 1:OWNERS], g_ss)
        all_in(relay_send.at[:, 1:SIDE], relay_ss)
        all_in(pack_recv, pack_ss)
        all_in(away_rows, away_ss)
        all_in(v_in, v_ss)
        put_v.wait()
        put_u.wait()

    finish()


def on_device(n_rows, user_factors, item_factors, ratings, user_offsets, item_offsets, counts):
    users, rank = user_factors.shape
    items = item_factors.shape[0]
    subs, entries = ratings.shape
    picked = OWNERS * TOUCH
    vmem = pl.BlockSpec(memory_space=pltpu.VMEM)
    hbm = pl.BlockSpec(memory_space=pl.ANY)
    dma = pltpu.SemaphoreType.DMA
    return pl.pallas_call(
        functools.partial(kernel, n_rows),
        out_shape=(
            pltpu.VMEM((users, rank), F32),
            pltpu.VMEM((items, rank), F32),
        ),
        in_specs=[hbm, hbm, vmem, vmem, vmem, vmem],
        out_specs=(hbm, hbm),
        scratch_shapes=[
            pltpu.VMEM((users, rank), F32),
            pltpu.VMEM((items, rank), F32),
            pltpu.VMEM((items, rank), F32),
            pltpu.VMEM((items, rank), F32),
            pltpu.VMEM((items, rank), BF16),
            pltpu.VMEM((items, rank), BF16),
            pltpu.VMEM((GROUPS, SIDE, 8, RUN), F32),
            pltpu.VMEM((OWNERS, 8, RUN), F32),
            pltpu.VMEM((8, 128), F32),
            pltpu.VMEM((8, entries), F32),
            pltpu.VMEM((picked, RUN), BF16),
            pltpu.VMEM((subs, RUN, picked), BF16),
            pltpu.VMEM((items, entries), BF16),
            pltpu.VMEM((items, entries), BF16),
            pltpu.VMEM((items, entries), BF16),
            pltpu.VMEM((subs + 1, picked, items), F32),
            pltpu.VMEM((subs + 1, picked, items), F32),
            pltpu.VMEM((picked, rank), BF16),
            pltpu.VMEM((picked, rank), BF16),
            pltpu.VMEM((picked, items), BF16),
            pltpu.VMEM((picked, items), BF16),
            pltpu.VMEM((OWNERS, TOUCH, rank), F32),
            pltpu.VMEM((subs, GROUPS, SIDE, TOUCH, rank), F32),
            pltpu.VMEM((subs, OWNERS, TOUCH, rank), F32),
            pltpu.VMEM((subs, OWNERS, TOUCH, rank), F32),
            pltpu.VMEM((2, users, rank), BF16),
            pltpu.VMEM((2, SIDE, SIDE, 8, RUN), F32),
            pltpu.VMEM((2, SIDE, users, rank // 2), F32),
            pltpu.VMEM((2, SIDE, SIDE, TOUCH, rank // 2), F32),
            pltpu.VMEM((8, entries), F32),
            pltpu.VMEM((8, entries), F32),
            pltpu.VMEM((GROUPS, SIDE, TOUCH, rank), F32),
            pltpu.VMEM((items, rank), BF16),
            pltpu.VMEM((items, rank), BF16),
            dma,
            dma,
            dma,
            dma((GROUPS,)),
            dma,
            dma,
            dma,
            dma((2,)),
            dma((2,)),
            dma((2, SIDE)),
            dma((2,)),
            dma,
            dma,
            dma,
            dma((GROUPS,)),
            dma,
            dma((subs, GROUPS)),
            dma,
            dma,
        ],
        compiler_params=pltpu.CompilerParams(
            collective_id=0, has_side_effects=True, vmem_limit_bytes=56 * 1024 * 1024
        ),
        name="sgd",
    )(user_factors, item_factors, ratings, user_offsets, item_offsets, counts.T)


def solution(mesh):
    shard = P(("rows", "strata"), None)
    split = P(None, ("rows", "strata"))
    return jax.shard_map(
        functools.partial(on_device, mesh.shape["rows"]),
        mesh=mesh,
        in_specs=(shard, shard, split, split, split, split),
        out_specs=(shard, shard),
        check_vma=False,
    )
```

```python
import functools

import jax
import jax.numpy as jnp
from jax import lax
from jax.experimental import pallas as pl
from jax.experimental.pallas import tpu as pltpu
from jax.sharding import PartitionSpec as P

MESH = pl.DeviceIdType.MESH
F32 = jnp.float32
BF16 = jnp.bfloat16

SIDE = 4
OWNERS = SIDE * SIDE
RUN = 128
TOUCH = 32
GROUPS = SIDE
STEPS = (0, 1, 3, 2)

NN = (((1,), (0,)), ((), ()))
NT = (((1,), (1,)), ((), ()))
TN = (((0,), (0,)), ((), ()))


def mm(a, b, dims):
    return lax.dot_general(a, b, dims, preferred_element_type=F32)


def halves(value):
    top = value.astype(BF16)
    return top, (value - top.astype(F32)).astype(BF16)


def mm3(a, b, dims):
    return mm(a[0], b[0], dims) + mm(a[0], b[1], dims) + mm(a[1], b[0], dims)


def iota(shape, dim):
    return lax.broadcasted_iota(jnp.int32, shape, dim)


def onehot(test):
    return jnp.where(test, 1.0, 0.0).astype(BF16)


def steps_of(sub_epoch):
    return 0.04 / (1.0 + 0.5 * sub_epoch)


def kernel(
    n_rows,
    u_hbm, v_hbm, rate_ref, user_ref, item_ref, count_ref,
    out_u, out_v,
    u_own, v_cur, v_in, v_new, v_hi, v_lo,
    mask_send, mask_recv, rank_tab, pos_tab,
    sel, sel_t,
    b_one, b_hi, b_lo, num, rat,
    ut_hi, ut_lo, w_hi, w_lo,
    u_send, u_recv, g_send, g_recv, u_parts,
    relay_mask, dense, relay_send,
    pack_send, pack_recv, away_rows, own_hi, own_lo,
    pack_ss, pack_rs, away_ss, away_rs,
    dense_ss, relay_ss, relay_ms, relay_mrs, dense_rs, relay_rs,
    load_sem, mask_ss, mask_rs, u_ss, u_rs, g_ss, g_rs, v_ss, v_rs,
):
    row = lax.axis_index("rows")
    place = lax.axis_index("strata")
    y, x = place // SIDE, place % SIDE
    up, down = (row + 1) % n_rows, (row + n_rows - 1) % n_rows
    items = v_cur.shape[0]
    entries = rate_ref.shape[1]
    subs = rate_ref.shape[0]

    def away(slot, sign):
        dy, dx = STEPS[slot // SIDE], slot % SIDE
        return ((y + sign * dy + SIDE) % SIDE) * SIDE + (x + sign * dx + SIDE) % SIDE

    def tile_of(slot):
        return (row, away(slot, 1))

    def owner_of(slot):
        return (row, away(slot, -1))

    barrier = pltpu.get_barrier_semaphore()
    for slot in range(1, OWNERS):
        pl.semaphore_signal(barrier, inc=1, device_id=tile_of(slot), device_id_type=MESH)
    for other in (up, down):
        pl.semaphore_signal(barrier, inc=1, device_id=(other, place), device_id_type=MESH)

    load_u = pltpu.make_async_copy(u_hbm, u_own, load_sem.at[0])
    load_v = pltpu.make_async_copy(v_hbm, v_cur, load_sem.at[1])
    load_u.start()
    load_v.start()

    def slot_and_run(t):
        user = user_ref[t : t + 1, :]
        owner = user >> 7
        dy = (y + SIDE - (owner >> 2)) & 3
        dx = (x + SIDE - (owner & 3)) & 3
        return (dy ^ (dy >> 1)) * SIDE + dx, user & (RUN - 1)

    for t in range(subs):
        slot_e, low_e = slot_and_run(t)
        hot_slot = onehot(iota((OWNERS, entries), 0) == slot_e)
        hot_low = onehot(iota((RUN, entries), 0) == low_e)
        named = jnp.where(mm(hot_slot, hot_low, NT) > 0.5, 1.0, 0.0)
        mask_send[:, :, t, :] = named.reshape(GROUPS, SIDE, RUN)
        before = onehot(iota((RUN, RUN), 0) < iota((RUN, RUN), 1))
        rank = mm(named.astype(BF16), before, NN)
        each = mm(rank.astype(BF16), hot_low, NN)
        rank_e = jnp.sum(jnp.where(iota((OWNERS, entries), 0) == slot_e, each, 0.0), axis=0, keepdims=True)
        pos_tab[t : t + 1, :] = slot_e.astype(F32) * float(TOUCH) + rank_e

    pack_send[0:1, :] = pos_tab[subs - 1 : subs, :]
    pack_send[1:2, :] = jnp.where(
        iota((1, entries), 1) < count_ref[0:1, subs - 1 : subs], item_ref[subs - 1 : subs, :], -1
    ).astype(F32)
    pack_send[2:3, :] = rate_ref[subs - 1 : subs, :]
    pl.semaphore_wait(barrier, OWNERS + 1)

    def mask_copy(slot):
        return pltpu.make_async_remote_copy(
            src_ref=mask_send.at[slot // SIDE, slot % SIDE], dst_ref=mask_recv.at[slot],
            send_sem=mask_ss, recv_sem=mask_rs,
            device_id=owner_of(slot), device_id_type=MESH)

    cut = u_own.shape[1] // 2
    HALVES = (slice(0, cut), slice(cut, 2 * cut))

    def u_copy(slot):
        return pltpu.make_async_remote_copy(
            src_ref=u_send.at[slot], dst_ref=u_recv.at[1, slot // SIDE, slot % SIDE],
            send_sem=u_ss, recv_sem=u_rs.at[slot // SIDE],
            device_id=tile_of(slot), device_id_type=MESH)

    def g_copy(t, slot):
        return pltpu.make_async_remote_copy(
            src_ref=g_send.at[t, slot], dst_ref=g_recv.at[t, slot],
            send_sem=g_ss, recv_sem=g_rs.at[t, slot // SIDE],
            device_id=owner_of(slot), device_id_type=MESH)

    def rows_in(t, group):
        if t:
            all_in(u_recv.at[t, group, (1 if group == 0 else 0) :], u_rs.at[group])
            return
        if group == 0:
            for step in range(1, SIDE):
                all_in(u_recv.at[0, :, step, :, HALVES[1]], relay_rs.at[1, step])
        else:
            all_in(u_recv.at[0, group, :, :, HALVES[0]], relay_rs.at[0, group])

    def grads_in(t, group):
        first = max(1, group * SIDE)
        all_in(g_recv.at[t, first : (group + 1) * SIDE], g_rs.at[t, group])

    def slots_of(group):
        return range(group * SIDE, (group + 1) * SIDE)

    def rows_of(group):
        return slice(group * RUN, (group + 1) * RUN)

    def named_items(t):
        active = iota((1, entries), 1) < count_ref[0:1, t : t + 1]
        return jnp.where(active, item_ref[t : t + 1, :], -1).astype(F32)

    def one_hot_items(t):
        if t < subs:
            rate, item = rate_ref[t : t + 1, :], named_items(t)
        else:
            rate, item = pack_recv[2:3, :], pack_recv[1:2, :]
        rate_top = rate.astype(BF16).astype(F32)
        rate_low = rate - rate_top
        step = 64

        def body(i, _):
            at = pl.ds(pl.multiple_of(i * step, step), step)
            hit = (iota((step, entries), 0) + i * step).astype(F32) == item
            b_one[at, :] = jnp.where(hit, 1.0, 0.0).astype(BF16)
            b_hi[at, :] = jnp.where(hit, rate_top, 0.0).astype(BF16)
            b_lo[at, :] = jnp.where(hit, rate_low, 0.0).astype(BF16)
            return 0

        lax.fori_loop(0, items // step, body, 0)

    def counts_and_ratings(t):
        pos = pos_tab[t : t + 1, :] if t < subs else pack_recv[0:1, :]

        def body(i, _):
            at = pl.ds(pl.multiple_of(i * RUN, RUN), RUN)
            here = (iota((RUN, entries), 0) + i * RUN).astype(F32)
            hot = onehot(here == pos)
            num[t, at, :] = mm(hot, b_one[...], NT)
            rat[t, at, :] = mm(hot, b_hi[...], NT) + mm(hot, b_lo[...], NT)
            return 0

        lax.fori_loop(0, GROUPS, body, 0)

    def split_v():
        top, low = halves(v_cur[...])
        v_hi[...] = top
        v_lo[...] = low


    def relay_place(hop, step, sign):
        dy, dx = (0, step) if hop == 0 else (STEPS[step], 0)
        return (row, ((y + sign * dy + SIDE) % SIDE) * SIDE + (x + sign * dx + SIDE) % SIDE)

    def dense_copy(hop, step):
        return pltpu.make_async_remote_copy(
            src_ref=u_own.at[:, HALVES[hop]], dst_ref=dense.at[hop, step],
            send_sem=dense_ss, recv_sem=dense_rs.at[hop],
            device_id=relay_place(hop, step, 1), device_id_type=MESH)

    def relay_mask_copy(hop, step):
        src = mask_send.at[step] if hop == 0 else mask_send.at[:, step]
        return pltpu.make_async_remote_copy(
            src_ref=src, dst_ref=relay_mask.at[hop, step],
            send_sem=relay_ms, recv_sem=relay_mrs.at[hop],
            device_id=relay_place(1 - hop, step, -1), device_id_type=MESH)

    def relay_copy(hop, step):
        cols = HALVES[hop]
        dst = u_recv.at[0, step, :, :, cols] if hop == 0 else u_recv.at[0, :, step, :, cols]
        return pltpu.make_async_remote_copy(
            src_ref=relay_send.at[hop, step], dst_ref=dst,
            send_sem=relay_ss, recv_sem=relay_rs.at[hop, step],
            device_id=relay_place(1 - hop, step, 1), device_id_type=MESH)

    def all_in(part, sem):
        pltpu.make_async_copy(part, part, sem).wait()

    def relay_out(hop):
        all_in(relay_mask.at[hop, 1:SIDE], relay_mrs.at[hop])
        if hop == 0:
            relay_mask[hop, 0] = mask_send[0]
        else:
            relay_mask[hop, 0] = mask_send[:, 0]
        mask = relay_mask[hop, :, :, 0, :].reshape(OWNERS, RUN)
        before = onehot(iota((RUN, RUN), 0) < iota((RUN, RUN), 1))
        rank = mm(mask.astype(BF16), before, NN)
        line = iota((OWNERS * TOUCH, OWNERS), 0)
        spread = onehot((line // TOUCH % SIDE) * SIDE + line // RUN == iota((OWNERS * TOUCH, OWNERS), 1))
        rank_rows = mm(spread, rank.astype(BF16), NN)
        mask_rows = mm(spread, mask.astype(BF16), NN)
        index = (iota((OWNERS * TOUCH, RUN), 0) % TOUCH).astype(F32)
        hit = jnp.where(rank_rows == index, mask_rows, 0.0).astype(BF16)
        all_in(dense.at[hop, 1:SIDE], dense_rs.at[hop])
        for step in range(SIDE):
            held = u_own[:, HALVES[hop]] if step == 0 else dense[hop, step]
            top, low = halves(held)
            hot = hit[step * RUN : (step + 1) * RUN, :]
            rows = mm(hot, top, NN) + mm(hot, low, NN)
            for to in range(SIDE):
                part = rows[to * TOUCH : (to + 1) * TOUCH, :]
                if to:
                    relay_send[hop, to, step] = part
                elif hop == 0:
                    u_recv[0, 0, step, :, HALVES[0]] = part
                else:
                    u_recv[0, step, 0, :, HALVES[1]] = part
        for to in range(1, SIDE):
            relay_copy(hop, to).start()

    def select_rows(t):
        mask = mask_recv[:, t, :]
        before = onehot(iota((RUN, RUN), 0) < iota((RUN, RUN), 1))
        rank = mm(mask.astype(BF16), before, NN)
        spread = onehot(iota((OWNERS * TOUCH, OWNERS), 0) // TOUCH == iota((OWNERS * TOUCH, OWNERS), 1))
        rank_rows = mm(spread, rank.astype(BF16), NN)
        mask_rows = mm(spread, mask.astype(BF16), NN)
        index = (iota((OWNERS * TOUCH, RUN), 0) % TOUCH).astype(F32)
        hit = jnp.where(rank_rows == index, mask_rows, 0.0)
        if t:
            sel[...] = hit.astype(BF16)
        sel_t[t] = hit.T.astype(BF16)

    def send_rows():
        for group in range(GROUPS):
            hot = sel[rows_of(group), :]
            rows = mm(hot, u_parts[0], NN) + mm(hot, u_parts[1], NN)
            for slot in slots_of(group):
                part = rows[(slot % SIDE) * TOUCH : (slot % SIDE + 1) * TOUCH, :]
                if slot:
                    u_send[slot] = part
                else:
                    u_recv[1, 0, 0] = part
            for slot in slots_of(group):
                if slot:
                    u_copy(slot).start()

    def away_copy(group):
        return pltpu.make_async_remote_copy(
            src_ref=u_recv.at[subs - 1, group], dst_ref=away_rows.at[group],
            send_sem=away_ss, recv_sem=away_rs.at[group],
            device_id=(down, place), device_id_type=MESH)

    def away_items():
        t = subs - 1
        own = (own_hi[...], own_lo[...])
        for group in range(GROUPS):
            all_in(away_rows.at[group], away_rs.at[group])
            at = rows_of(group)
            top, low = halves(away_rows[group].reshape(RUN, -1))
            ut_hi[at, :] = top
            ut_lo[at, :] = low
            w_top, w_low = halves(rat[subs, at, :] - num[subs, at, :] * mm3((top, low), own, NT))
            w_hi[at, :] = w_top
            w_lo[at, :] = w_low
        for chunk in range(items // RUN):
            at = slice(chunk * RUN, (chunk + 1) * RUN)
            old = v_new[at, :]
            v_cur[at, :] = old + steps_of(t) * (item_grad(0, GROUPS, chunk) - 0.1 * old)

    def tile_rows(t):
        for group in range(GROUPS):
            rows_in(t, group)
            if t + 1 == subs:
                away_copy(group).start()
            at = rows_of(group)
            top, low = halves(u_recv[t, group].reshape(RUN, -1))
            v = (v_hi[...], v_lo[...])
            w = rat[t, at, :] - num[t, at, :] * mm3((top, low), v, NT)
            w_top, w_low = halves(w)
            if t + 1 < subs:
                ut_hi[at, :] = top
                ut_lo[at, :] = low
                w_hi[at, :] = w_top
                w_lo[at, :] = w_low
            grad = mm3((w_top, w_low), v, NN)
            for slot in slots_of(group):
                part = grad[(slot % SIDE) * TOUCH : (slot % SIDE + 1) * TOUCH, :]
                if slot:
                    g_send[t, slot] = part
                else:
                    g_recv[t, slot] = part
            for slot in slots_of(group):
                if slot:
                    g_copy(t, slot).start()

    def user_step(t):
        old = u_own[...]
        total = jnp.zeros_like(old)
        for group in range(GROUPS):
            grads_in(t, group)
            top, low = halves(g_recv[t, group * SIDE : (group + 1) * SIDE].reshape(RUN, -1))
            back = sel_t[t, :, rows_of(group)]
            total = total + mm(back, top, NN) + mm(back, low, NN)
        u_own[...] = old + steps_of(t) * (total - 0.1 * old)

    def update_half():
        all_in(dense.at[:, 1:SIDE], dense_ss)
        user_step(0)
        top, low = halves(u_own[...])
        u_parts[0] = top
        u_parts[1] = low
        send_rows()

    def v_copy(chunk):
        at = pl.ds(chunk * RUN, RUN)
        return pltpu.make_async_remote_copy(
            src_ref=v_new.at[at], dst_ref=v_in.at[at],
            send_sem=v_ss, recv_sem=v_rs,
            device_id=(up, place), device_id_type=MESH)

    def item_grad(first, last, chunk):
        at = slice(chunk * RUN, (chunk + 1) * RUN)
        rows = slice(first * RUN, last * RUN)
        return mm3((w_hi[rows, at], w_lo[rows, at]), (ut_hi[rows, :], ut_lo[rows, :]), TN)

    def item_step_0():
        step = steps_of(0)
        for chunk in range(items // RUN):
            at = slice(chunk * RUN, (chunk + 1) * RUN)
            grad = item_grad(0, GROUPS, chunk)
            fresh = v_cur[at, :] + step * (grad - 0.1 * v_cur[at, :])
            v_new[at, :] = fresh
            v_copy(chunk).start()
            top, low = halves(fresh)
            own_hi[at, :] = top
            own_lo[at, :] = low

    load_u.wait()
    for step in range(1, SIDE):
        for hop in (1, 0):
            relay_mask_copy(hop, step).start()
    for step in (1, 3, 2):
        for hop in (1, 0):
            dense_copy(hop, step if hop == 0 else (0, 1, 3, 2)[step]).start()
    load_v.wait()
    split_v()
    one_hot_items(0)
    counts_and_ratings(0)
    relay_out(1)
    relay_out(0)
    for slot in range(1, OWNERS):
        mask_copy(slot).start()
    pack_copy = pltpu.make_async_remote_copy(
        src_ref=pack_send, dst_ref=pack_recv, send_sem=pack_ss, recv_sem=pack_rs,
        device_id=(down, place), device_id_type=MESH)
    pack_copy.start()
    mask_recv[0] = mask_send[0, 0]


    def wait_masks():
        all_in(mask_recv.at[1:OWNERS], mask_rs)

    tile_rows(0)
    item_step_0()
    wait_masks()
    select_rows(0)
    select_rows(1)
    one_hot_items(1)
    counts_and_ratings(1)
    update_half()

    def wait_v():
        all_in(v_in, v_rs)

    all_in(pack_recv, pack_rs)
    one_hot_items(2)
    counts_and_ratings(2)
    wait_v()
    top, low = halves(v_in[...])
    v_hi[...] = top
    v_lo[...] = low
    tile_rows(1)
    away_items()
    put_v = pltpu.make_async_copy(v_cur, out_v, load_sem.at[1])
    put_v.start()
    user_step(1)
    put_u = pltpu.make_async_copy(u_own, out_u, load_sem.at[0])
    put_u.start()

    def finish():
        all_in(mask_recv.at[1:OWNERS], mask_ss)
        all_in(relay_mask.at[:, 1:SIDE], relay_ms)
        all_in(u_send.at[1:OWNERS], u_ss)
        all_in(g_send.at[:, 1:OWNERS], g_ss)
        all_in(relay_send.at[:, 1:SIDE], relay_ss)
        all_in(pack_recv, pack_ss)
        all_in(away_rows, away_ss)
        all_in(v_in, v_ss)
        put_v.wait()
        put_u.wait()

    finish()


def on_device(n_rows, user_factors, item_factors, ratings, user_offsets, item_offsets, counts):
    users, rank = user_factors.shape
    items = item_factors.shape[0]
    subs, entries = ratings.shape
    picked = OWNERS * TOUCH
    vmem = pl.BlockSpec(memory_space=pltpu.VMEM)
    hbm = pl.BlockSpec(memory_space=pl.ANY)
    dma = pltpu.SemaphoreType.DMA
    return pl.pallas_call(
        functools.partial(kernel, n_rows),
        out_shape=(
            pltpu.VMEM((users, rank), F32),
            pltpu.VMEM((items, rank), F32),
        ),
        in_specs=[hbm, hbm, vmem, vmem, vmem, vmem],
        out_specs=(hbm, hbm),
        scratch_shapes=[
            pltpu.VMEM((users, rank), F32),
            pltpu.VMEM((items, rank), F32),
            pltpu.VMEM((items, rank), F32),
            pltpu.VMEM((items, rank), F32),
            pltpu.VMEM((items, rank), BF16),
            pltpu.VMEM((items, rank), BF16),
            pltpu.VMEM((GROUPS, SIDE, 8, RUN), F32),
            pltpu.VMEM((OWNERS, 8, RUN), F32),
            pltpu.VMEM((8, 128), F32),
            pltpu.VMEM((8, entries), F32),
            pltpu.VMEM((picked, RUN), BF16),
            pltpu.VMEM((subs, RUN, picked), BF16),
            pltpu.VMEM((items, entries), BF16),
            pltpu.VMEM((items, entries), BF16),
            pltpu.VMEM((items, entries), BF16),
            pltpu.VMEM((subs + 1, picked, items), F32),
            pltpu.VMEM((subs + 1, picked, items), F32),
            pltpu.VMEM((picked, rank), BF16),
            pltpu.VMEM((picked, rank), BF16),
            pltpu.VMEM((picked, items), BF16),
            pltpu.VMEM((picked, items), BF16),
            pltpu.VMEM((OWNERS, TOUCH, rank), F32),
            pltpu.VMEM((subs, GROUPS, SIDE, TOUCH, rank), F32),
            pltpu.VMEM((subs, OWNERS, TOUCH, rank), F32),
            pltpu.VMEM((subs, OWNERS, TOUCH, rank), F32),
            pltpu.VMEM((2, users, rank), BF16),
            pltpu.VMEM((2, SIDE, SIDE, 8, RUN), F32),
            pltpu.VMEM((2, SIDE, users, rank // 2), F32),
            pltpu.VMEM((2, SIDE, SIDE, TOUCH, rank // 2), F32),
            pltpu.VMEM((8, entries), F32),
            pltpu.VMEM((8, entries), F32),
            pltpu.VMEM((GROUPS, SIDE, TOUCH, rank), F32),
            pltpu.VMEM((items, rank), BF16),
            pltpu.VMEM((items, rank), BF16),
            dma,
            dma,
            dma,
            dma((GROUPS,)),
            dma,
            dma,
            dma,
            dma((2,)),
            dma((2,)),
            dma((2, SIDE)),
            dma((2,)),
            dma,
            dma,
            dma,
            dma((GROUPS,)),
            dma,
            dma((subs, GROUPS)),
            dma,
            dma,
        ],
        compiler_params=pltpu.CompilerParams(
            collective_id=0, has_side_effects=True, vmem_limit_bytes=56 * 1024 * 1024
        ),
        name="sgd",
    )(user_factors, item_factors, ratings, user_offsets, item_offsets, counts.T)


def solution(mesh):
    shard = P(("rows", "strata"), None)
    split = P(None, ("rows", "strata"))
    return jax.shard_map(
        functools.partial(on_device, mesh.shape["rows"]),
        mesh=mesh,
        in_specs=(shard, shard, split, split, split, split),
        out_specs=(shard, shard),
        check_vma=False,
    )
```

```python
import functools

import jax
import jax.numpy as jnp
from jax import lax
from jax.experimental import pallas as pl
from jax.experimental.pallas import tpu as pltpu
from jax.sharding import PartitionSpec as P

MESH = pl.DeviceIdType.MESH
F32 = jnp.float32
BF16 = jnp.bfloat16

SIDE = 4
OWNERS = SIDE * SIDE
RUN = 128
TOUCH = 32
GROUPS = SIDE
STEPS = (0, 1, 3, 2)

NN = (((1,), (0,)), ((), ()))
NT = (((1,), (1,)), ((), ()))
TN = (((0,), (0,)), ((), ()))


def mm(a, b, dims):
    return lax.dot_general(a, b, dims, preferred_element_type=F32)


def halves(value):
    top = value.astype(BF16)
    return top, (value - top.astype(F32)).astype(BF16)


def mm3(a, b, dims):
    return mm(a[0], b[0], dims) + mm(a[0], b[1], dims) + mm(a[1], b[0], dims)


def iota(shape, dim):
    return lax.broadcasted_iota(jnp.int32, shape, dim)


def onehot(test):
    return jnp.where(test, 1.0, 0.0).astype(BF16)


def steps_of(sub_epoch):
    return 0.04 / (1.0 + 0.5 * sub_epoch)


def kernel(
    n_rows,
    u_hbm, v_hbm, rate_ref, user_ref, item_ref, count_ref,
    out_u, out_v,
    u_own, v_cur, v_in, v_new, v_hi, v_lo,
    mask_send, mask_recv, rank_tab, pos_tab,
    sel, sel_t,
    b_one, b_hi, b_lo, num, rat,
    ut_hi, ut_lo, w_hi, w_lo,
    u_send, u_recv, g_send, g_recv, u_parts,
    relay_mask, dense, relay_send,
    pack_send, pack_recv, away_rows, own_hi, own_lo,
    pack_ss, pack_rs, away_ss, away_rs,
    dense_ss, relay_ss, relay_ms, relay_mrs, dense_rs, relay_rs,
    load_sem, mask_ss, mask_rs, u_ss, u_rs, g_ss, g_rs, v_ss, v_rs,
):
    row = lax.axis_index("rows")
    place = lax.axis_index("strata")
    y, x = place // SIDE, place % SIDE
    up, down = (row + 1) % n_rows, (row + n_rows - 1) % n_rows
    items = v_cur.shape[0]
    entries = rate_ref.shape[1]
    subs = rate_ref.shape[0]

    def away(slot, sign):
        dy, dx = STEPS[slot // SIDE], slot % SIDE
        return ((y + sign * dy + SIDE) % SIDE) * SIDE + (x + sign * dx + SIDE) % SIDE

    def tile_of(slot):
        return (row, away(slot, 1))

    def owner_of(slot):
        return (row, away(slot, -1))

    barrier = pltpu.get_barrier_semaphore()
    for slot in range(1, OWNERS):
        pl.semaphore_signal(barrier, inc=1, device_id=tile_of(slot), device_id_type=MESH)
    for other in (up, down):
        pl.semaphore_signal(barrier, inc=1, device_id=(other, place), device_id_type=MESH)

    load_u = pltpu.make_async_copy(u_hbm, u_own, load_sem.at[0])
    load_v = pltpu.make_async_copy(v_hbm, v_cur, load_sem.at[1])
    load_u.start()
    load_v.start()

    def slot_and_run(t):
        user = user_ref[t : t + 1, :]
        owner = user >> 7
        dy = (y + SIDE - (owner >> 2)) & 3
        dx = (x + SIDE - (owner & 3)) & 3
        return (dy ^ (dy >> 1)) * SIDE + dx, user & (RUN - 1)

    for t in range(subs):
        slot_e, low_e = slot_and_run(t)
        hot_slot = onehot(iota((OWNERS, entries), 0) == slot_e)
        hot_low = onehot(iota((RUN, entries), 0) == low_e)
        named = jnp.where(mm(hot_slot, hot_low, NT) > 0.5, 1.0, 0.0)
        mask_send[:, :, t, :] = named.reshape(GROUPS, SIDE, RUN)
        before = onehot(iota((RUN, RUN), 0) < iota((RUN, RUN), 1))
        rank = mm(named.astype(BF16), before, NN)
        each = mm(rank.astype(BF16), hot_low, NN)
        rank_e = jnp.sum(jnp.where(iota((OWNERS, entries), 0) == slot_e, each, 0.0), axis=0, keepdims=True)
        pos_tab[t : t + 1, :] = slot_e.astype(F32) * float(TOUCH) + rank_e

    pack_send[0:1, :] = pos_tab[subs - 1 : subs, :]
    pack_send[1:2, :] = jnp.where(
        iota((1, entries), 1) < count_ref[0:1, subs - 1 : subs], item_ref[subs - 1 : subs, :], -1
    ).astype(F32)
    pack_send[2:3, :] = rate_ref[subs - 1 : subs, :]
    pl.semaphore_wait(barrier, OWNERS + 1)

    def mask_copy(slot):
        return pltpu.make_async_remote_copy(
            src_ref=mask_send.at[slot // SIDE, slot % SIDE], dst_ref=mask_recv.at[slot],
            send_sem=mask_ss, recv_sem=mask_rs,
            device_id=owner_of(slot), device_id_type=MESH)

    cut = u_own.shape[1] // 2
    HALVES = (slice(0, cut), slice(cut, 2 * cut))

    def u_copy(slot):
        return pltpu.make_async_remote_copy(
            src_ref=u_send.at[slot], dst_ref=u_recv.at[1, slot // SIDE, slot % SIDE],
            send_sem=u_ss, recv_sem=u_rs.at[slot // SIDE],
            device_id=tile_of(slot), device_id_type=MESH)

    def g_copy(t, slot):
        return pltpu.make_async_remote_copy(
            src_ref=g_send.at[t, slot], dst_ref=g_recv.at[t, slot],
            send_sem=g_ss, recv_sem=g_rs.at[t, slot // SIDE],
            device_id=owner_of(slot), device_id_type=MESH)

    def rows_in(t, group):
        if t:
            all_in(u_recv.at[t, group, (1 if group == 0 else 0) :], u_rs.at[group])
            return
        if group == 0:
            for step in range(1, SIDE):
                all_in(u_recv.at[0, :, step, :, HALVES[1]], relay_rs.at[1, step])
        else:
            all_in(u_recv.at[0, group, :, :, HALVES[0]], relay_rs.at[0, group])

    def grads_in(t, group):
        first = max(1, group * SIDE)
        all_in(g_recv.at[t, first : (group + 1) * SIDE], g_rs.at[t, group])

    def slots_of(group):
        return [group * SIDE + step for step in STEPS]

    def rows_of(group):
        return slice(group * RUN, (group + 1) * RUN)

    def named_items(t):
        active = iota((1, entries), 1) < count_ref[0:1, t : t + 1]
        return jnp.where(active, item_ref[t : t + 1, :], -1).astype(F32)

    def one_hot_items(t):
        if t < subs:
            rate, item = rate_ref[t : t + 1, :], named_items(t)
        else:
            rate, item = pack_recv[2:3, :], pack_recv[1:2, :]
        rate_top = rate.astype(BF16).astype(F32)
        rate_low = rate - rate_top
        step = 64

        def body(i, _):
            at = pl.ds(pl.multiple_of(i * step, step), step)
            hit = (iota((step, entries), 0) + i * step).astype(F32) == item
            b_one[at, :] = jnp.where(hit, 1.0, 0.0).astype(BF16)
            b_hi[at, :] = jnp.where(hit, rate_top, 0.0).astype(BF16)
            b_lo[at, :] = jnp.where(hit, rate_low, 0.0).astype(BF16)
            return 0

        lax.fori_loop(0, items // step, body, 0)

    def counts_and_ratings(t):
        pos = pos_tab[t : t + 1, :] if t < subs else pack_recv[0:1, :]

        def body(i, _):
            at = pl.ds(pl.multiple_of(i * RUN, RUN), RUN)
            here = (iota((RUN, entries), 0) + i * RUN).astype(F32)
            hot = onehot(here == pos)
            num[t, at, :] = mm(hot, b_one[...], NT)
            rat[t, at, :] = mm(hot, b_hi[...], NT) + mm(hot, b_lo[...], NT)
            return 0

        lax.fori_loop(0, GROUPS, body, 0)

    def split_v():
        top, low = halves(v_cur[...])
        v_hi[...] = top
        v_lo[...] = low


    def relay_place(hop, step, sign):
        dy, dx = (0, step) if hop == 0 else (STEPS[step], 0)
        return (row, ((y + sign * dy + SIDE) % SIDE) * SIDE + (x + sign * dx + SIDE) % SIDE)

    def dense_copy(hop, step):
        return pltpu.make_async_remote_copy(
            src_ref=u_own.at[:, HALVES[hop]], dst_ref=dense.at[hop, step],
            send_sem=dense_ss, recv_sem=dense_rs.at[hop],
            device_id=relay_place(hop, step, 1), device_id_type=MESH)

    def relay_mask_copy(hop, step):
        src = mask_send.at[step] if hop == 0 else mask_send.at[:, step]
        return pltpu.make_async_remote_copy(
            src_ref=src, dst_ref=relay_mask.at[hop, step],
            send_sem=relay_ms, recv_sem=relay_mrs.at[hop],
            device_id=relay_place(1 - hop, step, -1), device_id_type=MESH)

    def relay_copy(hop, step):
        cols = HALVES[hop]
        dst = u_recv.at[0, step, :, :, cols] if hop == 0 else u_recv.at[0, :, step, :, cols]
        return pltpu.make_async_remote_copy(
            src_ref=relay_send.at[hop, step], dst_ref=dst,
            send_sem=relay_ss, recv_sem=relay_rs.at[hop, step],
            device_id=relay_place(1 - hop, step, 1), device_id_type=MESH)

    def all_in(part, sem):
        pltpu.make_async_copy(part, part, sem).wait()

    def relay_out(hop):
        all_in(relay_mask.at[hop, 1:SIDE], relay_mrs.at[hop])
        if hop == 0:
            relay_mask[hop, 0] = mask_send[0]
        else:
            relay_mask[hop, 0] = mask_send[:, 0]
        mask = relay_mask[hop, :, :, 0, :].reshape(OWNERS, RUN)
        before = onehot(iota((RUN, RUN), 0) < iota((RUN, RUN), 1))
        rank = mm(mask.astype(BF16), before, NN)
        line = iota((OWNERS * TOUCH, OWNERS), 0)
        spread = onehot((line // TOUCH % SIDE) * SIDE + line // RUN == iota((OWNERS * TOUCH, OWNERS), 1))
        rank_rows = mm(spread, rank.astype(BF16), NN)
        mask_rows = mm(spread, mask.astype(BF16), NN)
        index = (iota((OWNERS * TOUCH, RUN), 0) % TOUCH).astype(F32)
        hit = jnp.where(rank_rows == index, mask_rows, 0.0).astype(BF16)
        all_in(dense.at[hop, 1:SIDE], dense_rs.at[hop])
        for step in range(SIDE):
            held = u_own[:, HALVES[hop]] if step == 0 else dense[hop, step]
            top, low = halves(held)
            hot = hit[step * RUN : (step + 1) * RUN, :]
            rows = mm(hot, top, NN) + mm(hot, low, NN)
            for to in range(SIDE):
                part = rows[to * TOUCH : (to + 1) * TOUCH, :]
                if to:
                    relay_send[hop, to, step] = part
                elif hop == 0:
                    u_recv[0, 0, step, :, HALVES[0]] = part
                else:
                    u_recv[0, step, 0, :, HALVES[1]] = part
        for to in range(1, SIDE):
            relay_copy(hop, to).start()

    def select_rows(t):
        mask = mask_recv[:, t, :]
        before = onehot(iota((RUN, RUN), 0) < iota((RUN, RUN), 1))
        rank = mm(mask.astype(BF16), before, NN)
        spread = onehot(iota((OWNERS * TOUCH, OWNERS), 0) // TOUCH == iota((OWNERS * TOUCH, OWNERS), 1))
        rank_rows = mm(spread, rank.astype(BF16), NN)
        mask_rows = mm(spread, mask.astype(BF16), NN)
        index = (iota((OWNERS * TOUCH, RUN), 0) % TOUCH).astype(F32)
        hit = jnp.where(rank_rows == index, mask_rows, 0.0)
        if t:
            sel[...] = hit.astype(BF16)
        sel_t[t] = hit.T.astype(BF16)

    def send_rows():
        for group in range(GROUPS):
            hot = sel[rows_of(group), :]
            rows = mm(hot, u_parts[0], NN) + mm(hot, u_parts[1], NN)
            for slot in slots_of(group):
                part = rows[(slot % SIDE) * TOUCH : (slot % SIDE + 1) * TOUCH, :]
                if slot:
                    u_send[slot] = part
                else:
                    u_recv[1, 0, 0] = part
            for slot in slots_of(group):
                if slot:
                    u_copy(slot).start()

    def away_copy(group):
        return pltpu.make_async_remote_copy(
            src_ref=u_recv.at[subs - 1, group], dst_ref=away_rows.at[group],
            send_sem=away_ss, recv_sem=away_rs.at[group],
            device_id=(down, place), device_id_type=MESH)

    def away_items():
        t = subs - 1
        own = (own_hi[...], own_lo[...])
        for group in range(GROUPS):
            all_in(away_rows.at[group], away_rs.at[group])
            at = rows_of(group)
            top, low = halves(away_rows[group].reshape(RUN, -1))
            ut_hi[at, :] = top
            ut_lo[at, :] = low
            w_top, w_low = halves(rat[subs, at, :] - num[subs, at, :] * mm3((top, low), own, NT))
            w_hi[at, :] = w_top
            w_lo[at, :] = w_low
        for chunk in range(items // RUN):
            at = slice(chunk * RUN, (chunk + 1) * RUN)
            old = v_new[at, :]
            v_cur[at, :] = old + steps_of(t) * (item_grad(0, GROUPS, chunk) - 0.1 * old)

    def tile_rows(t):
        for group in range(GROUPS):
            rows_in(t, group)
            if t + 1 == subs:
                away_copy(group).start()
            at = rows_of(group)
            top, low = halves(u_recv[t, group].reshape(RUN, -1))
            v = (v_hi[...], v_lo[...])
            w = rat[t, at, :] - num[t, at, :] * mm3((top, low), v, NT)
            w_top, w_low = halves(w)
            if t + 1 < subs:
                ut_hi[at, :] = top
                ut_lo[at, :] = low
                w_hi[at, :] = w_top
                w_lo[at, :] = w_low
            grad = mm3((w_top, w_low), v, NN)
            for slot in slots_of(group):
                part = grad[(slot % SIDE) * TOUCH : (slot % SIDE + 1) * TOUCH, :]
                if slot:
                    g_send[t, slot] = part
                else:
                    g_recv[t, slot] = part
            for slot in slots_of(group):
                if slot:
                    g_copy(t, slot).start()

    def user_step(t):
        old = u_own[...]
        total = jnp.zeros_like(old)
        for group in range(GROUPS):
            grads_in(t, group)
            top, low = halves(g_recv[t, group * SIDE : (group + 1) * SIDE].reshape(RUN, -1))
            back = sel_t[t, :, rows_of(group)]
            total = total + mm(back, top, NN) + mm(back, low, NN)
        u_own[...] = old + steps_of(t) * (total - 0.1 * old)

    def update_half():
        all_in(dense.at[:, 1:SIDE], dense_ss)
        user_step(0)
        top, low = halves(u_own[...])
        u_parts[0] = top
        u_parts[1] = low
        send_rows()

    def v_copy(chunk):
        at = pl.ds(chunk * RUN, RUN)
        return pltpu.make_async_remote_copy(
            src_ref=v_new.at[at], dst_ref=v_in.at[at],
            send_sem=v_ss, recv_sem=v_rs,
            device_id=(up, place), device_id_type=MESH)

    def item_grad(first, last, chunk):
        at = slice(chunk * RUN, (chunk + 1) * RUN)
        rows = slice(first * RUN, last * RUN)
        return mm3((w_hi[rows, at], w_lo[rows, at]), (ut_hi[rows, :], ut_lo[rows, :]), TN)

    def item_step_0():
        step = steps_of(0)
        for chunk in range(items // RUN):
            at = slice(chunk * RUN, (chunk + 1) * RUN)
            grad = item_grad(0, GROUPS, chunk)
            fresh = v_cur[at, :] + step * (grad - 0.1 * v_cur[at, :])
            v_new[at, :] = fresh
            v_copy(chunk).start()
            top, low = halves(fresh)
            own_hi[at, :] = top
            own_lo[at, :] = low

    load_u.wait()
    for step in range(1, SIDE):
        for hop in (1, 0):
            relay_mask_copy(hop, step).start()
    for step in (1, 3, 2):
        for hop in (1, 0):
            dense_copy(hop, step if hop == 0 else (0, 1, 3, 2)[step]).start()
    load_v.wait()
    split_v()
    one_hot_items(0)
    counts_and_ratings(0)
    relay_out(1)
    relay_out(0)
    for slot in range(1, OWNERS):
        mask_copy(slot).start()
    pack_copy = pltpu.make_async_remote_copy(
        src_ref=pack_send, dst_ref=pack_recv, send_sem=pack_ss, recv_sem=pack_rs,
        device_id=(down, place), device_id_type=MESH)
    pack_copy.start()
    mask_recv[0] = mask_send[0, 0]


    def wait_masks():
        all_in(mask_recv.at[1:OWNERS], mask_rs)

    tile_rows(0)
    item_step_0()
    wait_masks()
    select_rows(0)
    select_rows(1)
    one_hot_items(1)
    counts_and_ratings(1)
    update_half()

    def wait_v():
        all_in(v_in, v_rs)

    all_in(pack_recv, pack_rs)
    one_hot_items(2)
    counts_and_ratings(2)
    wait_v()
    top, low = halves(v_in[...])
    v_hi[...] = top
    v_lo[...] = low
    tile_rows(1)
    away_items()
    put_v = pltpu.make_async_copy(v_cur, out_v, load_sem.at[1])
    put_v.start()
    user_step(1)
    put_u = pltpu.make_async_copy(u_own, out_u, load_sem.at[0])
    put_u.start()

    def finish():
        all_in(mask_recv.at[1:OWNERS], mask_ss)
        all_in(relay_mask.at[:, 1:SIDE], relay_ms)
        all_in(u_send.at[1:OWNERS], u_ss)
        all_in(g_send.at[:, 1:OWNERS], g_ss)
        all_in(relay_send.at[:, 1:SIDE], relay_ss)
        all_in(pack_recv, pack_ss)
        all_in(away_rows, away_ss)
        all_in(v_in, v_ss)
        put_v.wait()
        put_u.wait()

    finish()


def on_device(n_rows, user_factors, item_factors, ratings, user_offsets, item_offsets, counts):
    users, rank = user_factors.shape
    items = item_factors.shape[0]
    subs, entries = ratings.shape
    picked = OWNERS * TOUCH
    vmem = pl.BlockSpec(memory_space=pltpu.VMEM)
    hbm = pl.BlockSpec(memory_space=pl.ANY)
    dma = pltpu.SemaphoreType.DMA
    return pl.pallas_call(
        functools.partial(kernel, n_rows),
        out_shape=(
            pltpu.VMEM((users, rank), F32),
            pltpu.VMEM((items, rank), F32),
        ),
        in_specs=[hbm, hbm, vmem, vmem, vmem, vmem],
        out_specs=(hbm, hbm),
        scratch_shapes=[
            pltpu.VMEM((users, rank), F32),
            pltpu.VMEM((items, rank), F32),
            pltpu.VMEM((items, rank), F32),
            pltpu.VMEM((items, rank), F32),
            pltpu.VMEM((items, rank), BF16),
            pltpu.VMEM((items, rank), BF16),
            pltpu.VMEM((GROUPS, SIDE, 8, RUN), F32),
            pltpu.VMEM((OWNERS, 8, RUN), F32),
            pltpu.VMEM((8, 128), F32),
            pltpu.VMEM((8, entries), F32),
            pltpu.VMEM((picked, RUN), BF16),
            pltpu.VMEM((subs, RUN, picked), BF16),
            pltpu.VMEM((items, entries), BF16),
            pltpu.VMEM((items, entries), BF16),
            pltpu.VMEM((items, entries), BF16),
            pltpu.VMEM((subs + 1, picked, items), F32),
            pltpu.VMEM((subs + 1, picked, items), F32),
            pltpu.VMEM((picked, rank), BF16),
            pltpu.VMEM((picked, rank), BF16),
            pltpu.VMEM((picked, items), BF16),
            pltpu.VMEM((picked, items), BF16),
            pltpu.VMEM((OWNERS, TOUCH, rank), F32),
            pltpu.VMEM((subs, GROUPS, SIDE, TOUCH, rank), F32),
            pltpu.VMEM((subs, OWNERS, TOUCH, rank), F32),
            pltpu.VMEM((subs, OWNERS, TOUCH, rank), F32),
            pltpu.VMEM((2, users, rank), BF16),
            pltpu.VMEM((2, SIDE, SIDE, 8, RUN), F32),
            pltpu.VMEM((2, SIDE, users, rank // 2), F32),
            pltpu.VMEM((2, SIDE, SIDE, TOUCH, rank // 2), F32),
            pltpu.VMEM((8, entries), F32),
            pltpu.VMEM((8, entries), F32),
            pltpu.VMEM((GROUPS, SIDE, TOUCH, rank), F32),
            pltpu.VMEM((items, rank), BF16),
            pltpu.VMEM((items, rank), BF16),
            dma,
            dma,
            dma,
            dma((GROUPS,)),
            dma,
            dma,
            dma,
            dma((2,)),
            dma((2,)),
            dma((2, SIDE)),
            dma((2,)),
            dma,
            dma,
            dma,
            dma((GROUPS,)),
            dma,
            dma((subs, GROUPS)),
            dma,
            dma,
        ],
        compiler_params=pltpu.CompilerParams(
            collective_id=0, has_side_effects=True, vmem_limit_bytes=56 * 1024 * 1024
        ),
        name="sgd",
    )(user_factors, item_factors, ratings, user_offsets, item_offsets, counts.T)


def solution(mesh):
    shard = P(("rows", "strata"), None)
    split = P(None, ("rows", "strata"))
    return jax.shard_map(
        functools.partial(on_device, mesh.shape["rows"]),
        mesh=mesh,
        in_specs=(shard, shard, split, split, split, split),
        out_specs=(shard, shard),
        check_vma=False,
    )
```
